32 devices in a mesh: ri: 8 (over z, core), rj: 4 (over y, x).
Axes of the slice: x: 2, y: 2, z: 4, core: 2. Of those that a mesh axis runs over, the one named last changes fastest.
Arguments:
- pair: bfloat16 [320, 320, 128], P('ri', 'rj'), may hold values from -6 to 6
- in_gain: float32 [128], replicated, may hold values from 0.1 to 1.9
- in_bias: float32 [128], replicated, may hold values from -3 to 3
- w_in: bfloat16 [128, 512], replicated, may hold values from -0.5 to 0.5
- w_gate: bfloat16 [128, 128], replicated, may hold values from -0.5 to 0.5
- out_gain: float32 [128], replicated, may hold values from 0.1 to 1.9
- out_bias: float32 [128], replicated, may hold values from -3 to 3
- w_out: bfloat16 [128, 128], replicated, may hold values from -0.5 to 0.5
Outputs:
- update: bfloat16 [320, 320, 128], P('ri', 'rj')
The draws below stay inside these ranges and needn't reach their ends.
All inputs are finite; a program needn't handle non-finite values.
Results may differ from the reference program's by a relative error of at most 0.015.
Values may be sent and summed in bfloat16 or wider, within the bound.
A program may use at most 128 MiB of HBM per device.

```python
import jax
import jax.numpy as jnp
from jax import lax

C = 128
H = 128
NR = 320


def steps_of(own_key, extent, shards, least, top_value):
    level, own = 1.0, jax.random.fold_in(own_key, 6)
    for dim, parts in shards:
        steps = jnp.exp(jax.random.uniform(jax.random.fold_in(own, dim), (parts,), jnp.float32, least / len(shards), top_value / len(shards)))
        level = level * jnp.repeat(steps, extent[dim] // parts).reshape([-1 if axis == dim else 1 for axis in range(len(extent))])
    return level


def normal_values(stream_key, shape, width, bound, cuts=(), dtype=jnp.bfloat16):
    level = steps_of(stream_key, shape, cuts, -0.22, 0.18) if cuts else 1.0
    drawn = jax.random.normal(stream_key, shape, jnp.float32) * width * level
    return jnp.minimum(jnp.maximum(drawn, -bound), bound).astype(dtype)


def setup_inputs(seed: int = 0) -> dict:
    splits = jax.random.split(jax.random.key(seed), 9)
    pair = normal_values(splits[0], (NR, NR, C), 1.0, 6.0, ((0, 8), (1, 4)))
    in_gain = jnp.clip(1.0 + 0.18 * jax.random.normal(splits[1], (C,), jnp.float32), 0.1, 1.9)
    in_bias = normal_values(splits[2], (C,), 0.5, 3.0, (), jnp.float32)
    w_in = normal_values(splits[3], (C, 4 * H), C ** -0.5, 0.5)
    w_gate = normal_values(splits[4], (C, C), C ** -0.5, 0.5)
    out_gain = jnp.clip(1.0 + 0.18 * jax.random.normal(splits[5], (H,), jnp.float32), 0.1, 1.9)
    out_bias = normal_values(splits[6], (H,), 0.5, 3.0, (), jnp.float32)
    w_out = normal_values(splits[7], (H, C), H ** -0.5, 0.5)
    return dict(pair=pair, in_gain=in_gain, in_bias=in_bias, w_in=w_in, w_gate=w_gate, out_gain=out_gain, out_bias=out_bias, w_out=w_out)


def layer_norm(values, gain, bias):
    mean = lax.optimization_barrier(jnp.mean(values, axis=-1, keepdims=True))
    centered = values - mean
    var = lax.optimization_barrier(jnp.mean(centered * centered, axis=-1, keepdims=True))
    return centered * lax.rsqrt(var + 1e-05) * gain + bias

def reference(pair, in_gain, in_bias, w_in, w_gate, out_gain, out_bias, w_out):
    normed = layer_norm(pair.astype(jnp.float32), in_gain, in_bias).astype(jnp.bfloat16)
    flat = normed.reshape(NR * NR, C)
    proj = jnp.dot(flat, w_in, preferred_element_type=jnp.float32)
    a_vals = (jax.nn.sigmoid(proj[:, H:2 * H]) * proj[:, :H]).astype(jnp.bfloat16).reshape(NR, NR, H)
    b_vals = (jax.nn.sigmoid(proj[:, 3 * H:]) * proj[:, 2 * H:3 * H]).astype(jnp.bfloat16).reshape(NR, NR, H)
    gate = jax.nn.sigmoid(jnp.dot(flat, w_gate, preferred_element_type=jnp.float32)).astype(jnp.bfloat16)
    tri = jnp.einsum('kic,kjc->ijc', a_vals.astype(jnp.float32), b_vals.astype(jnp.float32))
    tri_normed = layer_norm(tri, out_gain, out_bias).astype(jnp.bfloat16).reshape(NR * NR, H)
    mixed = jnp.dot(tri_normed, w_out, preferred_element_type=jnp.float32)
    update = gate.astype(jnp.float32) * mixed
    return update.reshape(NR, NR, C).astype(jnp.bfloat16)
```

```python
import functools

import jax
import jax.numpy as jnp
from jax import lax
from jax.experimental import pallas as pl
from jax.experimental.pallas import tpu as pltpu
from jax.sharding import PartitionSpec as P

MESH = pl.DeviceIdType.MESH
LANES = 128
STEPS = 5


def plan(n_ri, n_rj, hidden):
    team = n_ri * n_rj // 2
    per = hidden // team
    if per == 8 and n_ri % 4 == 0:
        sizes = [(2, False), (2, False), (4, False)]
    elif per > 1:
        sizes = [(per // 2, False)] * 2
    else:
        sizes = [(per, False)]
    parts, base = [], 0
    for own, inner in sizes:
        owners = team // 2 if inner else team
        parts.append((own, base, owners, inner))
        base += own * owners
    return parts


def shifted(vregs, start):
    at, by = divmod(start, LANES)
    if by == 0:
        return vregs[at]
    return pltpu.roll(vregs[at], LANES - by, 1)


def body(n_ri, n_rj, rows, cols, parts, *refs):
    np_ = len(parts)
    pair, gain, bias, w_in, w_gate, out_gain, out_bias, w_out, upd_ref = refs[:9]
    flat_s, ab_s, gate_s, tri_s, g_s, b_s, o_s = refs[9:16]
    x_s, recv_s, t_s, got_s = (refs[16 + i * np_ : 16 + (i + 1) * np_] for i in range(4))
    send1, recv1, send2, recv2, loc = refs[16 + 4 * np_ :]

    n = n_ri * n_rj
    spots = rows * cols
    side = n_ri // 2
    team = n // 2
    depth = side * rows
    hidden = tri_s.shape[0]
    halves = cols // rows
    ri, rj = lax.axis_index("ri"), lax.axis_index("rj")
    me = ri * n_rj + rj
    seat = lax.rem(ri, side) * n_rj + rj
    base = (ri // side) * side
    half = ri // side
    low = jnp.where(half == 0, side // 2, 0)
    inner_seat = seat - low * n_rj
    is_inner = jnp.logical_and(inner_seat >= 0, inner_seat < team // 2)

    def other(d):
        return lax.rem(me + d, n)

    barrier = pltpu.get_barrier_semaphore()
    pl.semaphore_signal(
        barrier, inc=1, device_id=(lax.rem(ri + side, n_ri), rj), device_id_type=MESH
    )

    def greet(d, _):
        to = lax.rem(seat + team - d, team)
        pl.semaphore_signal(
            barrier, inc=1, device_id=(base + to // n_rj, lax.rem(to, n_rj)), device_id_type=MESH
        )
        return _

    lax.fori_loop(1, team, greet, 0)

    wt = w_in[...].T
    step = spots // STEPS

    def norm_in(i, _):
        at = pl.multiple_of(i * step, LANES)
        x = pair[pl.ds(at, step), :].astype(jnp.float32)
        mean = jnp.mean(x, axis=-1, keepdims=True)
        centered = x - mean
        var = jnp.mean(centered * centered, axis=-1, keepdims=True)
        flat = (centered * lax.rsqrt(var + 1e-05) * gain[...] + bias[...]).astype(jnp.bfloat16)
        flat_s[pl.ds(at, step), :] = flat
        return _

    lax.fori_loop(0, STEPS, norm_in, 0)

    def owner_of(t, e):
        if parts[t][3]:
            return base + low + e // n_rj, lax.rem(e, n_rj)
        return base + e // n_rj, lax.rem(e, n_rj)

    def owner_seat(t):
        return inner_seat if parts[t][3] else seat

    def owns(t, f):
        if parts[t][3]:
            pl.when(is_inner)(f)
        else:
            f()

    def copy_in(t, e, src):
        return pltpu.make_async_remote_copy(
            src_ref=x_s[t].at[e], dst_ref=recv_s[t].at[src], send_sem=send1.at[t, e],
            recv_sem=recv1.at[t, src], device_id=owner_of(t, e), device_id_type=MESH,
        )

    def copy_back(t, d, src):
        return pltpu.make_async_remote_copy(
            src_ref=t_s[t].at[d], dst_ref=got_s[t].at[src], send_sem=send2.at[t, d],
            recv_sem=recv2.at[t, src], device_id=(d // n_rj, lax.rem(d, n_rj)),
            device_id_type=MESH,
        )

    def slot(t, h, e):
        return h * parts[t][2] + e

    def my_slot(t):
        return slot(t, half, owner_seat(t))

    def project(t):
        own, first, owners, _ = parts[t]
        wide = own * owners
        each = 8 // own
        w = jnp.concatenate(
            [wt[g * hidden + first : g * hidden + first + wide] for g in range(4)], axis=0
        )

        def one(i, _):
            at = pl.multiple_of(i * step, LANES)
            proj = lax.dot_general(
                w, flat_s[pl.ds(at, step), :], (((1,), (1,)), ((), ())),
                preferred_element_type=jnp.float32,
            )
            ab_s[0, :wide, pl.ds(at, step)] = jax.nn.sigmoid(proj[wide : 2 * wide]) * proj[:wide]
            ab_s[1, :wide, pl.ds(at, step)] = (
                jax.nn.sigmoid(proj[3 * wide :]) * proj[2 * wide : 3 * wide]
            )
            return _

        lax.fori_loop(0, STEPS, one, 0)

        def split(p, _):
            at = pl.multiple_of(p * 8, 8)
            a8, b8 = ab_s[0, pl.ds(at, 8), :], ab_s[1, pl.ds(at, 8), :]
            for e in range(each):
                pick = slice(e * own, (e + 1) * own)
                x_s[t][p * each + e] = jnp.concatenate([a8[pick], b8[pick]], axis=0).astype(
                    jnp.bfloat16
                )
            return _

        lax.fori_loop(0, wide // 8, split, 0)

    def others(t, f):
        owners, mine = parts[t][2], owner_seat(t)

        def one(d, _):
            e = lax.rem(seat + d, owners)

            @pl.when(e != mine)
            def go():
                f(e)

            return _

        lax.fori_loop(0, owners, one, 0)

    for t in range(np_):
        project(t)
        if t == 0:
            pl.semaphore_wait(barrier, team)
        others(t, lambda e, t=t: copy_in(t, e, seat).start())

    def gates(i, _):
        at = pl.multiple_of(i * step, LANES)
        gate_s[pl.ds(at, step), :] = jax.nn.sigmoid(
            jnp.dot(flat_s[pl.ds(at, step), :], w_gate[...], preferred_element_type=jnp.float32)
        ).astype(jnp.bfloat16)
        return _

    lax.fori_loop(0, STEPS, gates, 0)

    def work(t):
        own = parts[t][0]
        lane = lax.broadcasted_iota(jnp.int32, (2 * own, LANES), 1)
        lane_o = lax.broadcasted_iota(jnp.int32, (own, LANES), 1)

        def unpack(block, src):
            i0 = (src // n_rj) * rows
            j = lax.rem(src, n_rj)
            wide = block.astype(jnp.float32)
            vregs = [wide[:, v * LANES : (v + 1) * LANES] for v in range(spots // LANES)]
            for k in range(rows):
                start = k * cols
                val = shifted(vregs, start)
                have = LANES - start % LANES
                if have < cols:
                    val = jnp.where(
                        lane < have, val, pltpu.roll(vregs[start // LANES + 1], have, 1)
                    )
                g_s[j, pl.ds(i0 + k, 2 * own, stride=depth), :] = val

        unpack(x_s[t][owner_seat(t)], seat)

        def take(d, _):
            src = lax.rem(seat + team - d, team)
            copy_in(t, 0, src).wait_recv()
            unpack(recv_s[t][src], src)
            return _

        lax.fori_loop(1, team, take, 0)

        for c in range(own):
            for q in range(n_rj):
                b_s[c, :, q * LANES : (q + 1) * LANES] = g_s[
                    q, (own + c) * depth : (own + c + 1) * depth, :
                ].astype(jnp.bfloat16)

        def emit(pp, _):
            p = lax.rem(pp + n_rj // 2 + ri // halves, n_rj)
            for c in range(own):
                lhs = g_s[p, c * depth : (c + 1) * depth, :].astype(jnp.bfloat16)
                product = lax.dot_general(
                    lhs, b_s[c], (((0,), (0,)), ((), ())), preferred_element_type=jnp.float32
                )
                for q in range(n_rj):
                    o_s[q, c * LANES : (c + 1) * LANES, :] = product[:, q * LANES : (q + 1) * LANES]

            def deliver(s, _):
                h, q = s // n_rj, lax.rem(s + rj, n_rj)
                d = (p * halves + h) * n_rj + q
                got = [
                    o_s[q, pl.ds(h * rows + r, own, stride=LANES), :] for r in range(rows)
                ]
                pieces = []
                for v in range(spots // LANES):
                    piece = None
                    for r in range(
                        (v * LANES) // cols, min(rows, ((v + 1) * LANES - 1) // cols + 1)
                    ):
                        at = r * cols - v * LANES
                        val = pltpu.roll(got[r], at % LANES, 1) if at % LANES else got[r]
                        piece = val if piece is None else jnp.where(lane_o >= at, val, piece)
                    pieces.append(piece)
                t_s[t][d] = jnp.concatenate(pieces, axis=1).astype(jnp.bfloat16)

                @pl.when(d != me)
                def start():
                    copy_back(t, d, my_slot(t)).start()

                return _

            lax.fori_loop(0, halves * n_rj, deliver, 0)
            return _

        lax.fori_loop(0, n_rj, emit, 0)
        pltpu.make_async_copy(t_s[t].at[me], got_s[t].at[my_slot(t)], loc.at[t]).start()

    for t in range(np_):
        owns(t, lambda t=t: work(t))

    for t in range(np_):
        own, first, owners, inner = parts[t]
        each = 8 // own
        others(t, lambda e, t=t: copy_in(t, e, seat).wait_send())

        def drain(t=t):
            def sent(d, _):
                copy_back(t, other(d), my_slot(t)).wait_send()
                return _

            lax.fori_loop(1, n, sent, 0)
            pltpu.make_async_copy(t_s[t].at[me], got_s[t].at[my_slot(t)], loc.at[t]).wait()

        owns(t, drain)
        mine = my_slot(t)
        owned = is_inner if inner else None

        def arrive(s, _, t=t):
            go = s != mine if owned is None else jnp.logical_or(s != mine, jnp.logical_not(owned))

            @pl.when(go)
            def wait():
                copy_back(t, 0, s).wait_recv()

            return _

        lax.fori_loop(0, 2 * owners, arrive, 0)

        def merge(p, _, t=t):
            at = pl.multiple_of(first + p * 8, 8)
            sums = [
                got_s[t][p * each + e].astype(jnp.float32)
                + got_s[t][owners + p * each + e].astype(jnp.float32)
                for e in range(each)
            ]
            tri_s[pl.ds(at, 8), :] = jnp.concatenate(sums, axis=0)
            return _

        lax.fori_loop(0, own * owners // 8, merge, 0)

    def column(row):
        tall = jnp.broadcast_to(row[...], (LANES, hidden)).T
        return jnp.concatenate([tall] * (step // LANES), axis=1)

    post_gain, post_bias = column(out_gain), column(out_bias)

    def finish(i, _):
        at = pl.multiple_of(i * step, LANES)
        x = tri_s[:, pl.ds(at, step)]
        mean = jnp.mean(x, axis=0, keepdims=True)
        centered = x - mean
        var = jnp.mean(centered * centered, axis=0, keepdims=True)
        normed = (centered * lax.rsqrt(var + 1e-05) * post_gain + post_bias).astype(
            jnp.bfloat16
        )
        mixed = lax.dot_general(
            normed, w_out[...], (((0,), (0,)), ((), ())), preferred_element_type=jnp.float32
        )
        upd_ref[pl.ds(at, step), :] = (
            gate_s[pl.ds(at, step), :].astype(jnp.float32) * mixed
        ).astype(jnp.bfloat16)
        return _

    lax.fori_loop(0, STEPS, finish, 0)


def local(n_ri, n_rj, pair, in_gain, in_bias, w_in, w_gate, out_gain, out_bias, w_out):
    rows, cols, chans = pair.shape
    hidden = w_out.shape[0]
    n = n_ri * n_rj
    team = n // 2
    spots = rows * cols
    depth = (n_ri // 2) * rows
    parts = plan(n_ri, n_rj, hidden)
    most = max(own for own, *_ in parts)
    wide = max(own * owners for own, _, owners, _ in parts)
    vmem = pl.BlockSpec(memory_space=pltpu.VMEM)
    bf16, f32 = jnp.bfloat16, jnp.float32
    k = len(parts)
    update = pl.pallas_call(
        functools.partial(body, n_ri, n_rj, rows, cols, parts),
        out_shape=jax.ShapeDtypeStruct((spots, w_out.shape[1]), bf16),
        in_specs=[vmem] * 8,
        out_specs=vmem,
        scratch_shapes=[
            pltpu.VMEM((spots, chans), bf16),
            pltpu.VMEM((2, wide, spots), f32),
            pltpu.VMEM((spots, chans), bf16),
            pltpu.VMEM((hidden, spots), f32),
            pltpu.VMEM((n_rj, 2 * most * depth, LANES), f32),
            pltpu.VMEM((most, depth, n_rj * LANES), bf16),
            pltpu.VMEM((n_rj, most * LANES, LANES), f32),
            *[pltpu.VMEM((owners, 2 * own, spots), bf16) for own, _, owners, _ in parts],
            *[pltpu.VMEM((team, 2 * own, spots), bf16) for own, _, owners, _ in parts],
            *[pltpu.VMEM((n, own, spots), bf16) for own, _, owners, _ in parts],
            *[pltpu.VMEM((2 * owners, own, spots), bf16) for own, _, owners, _ in parts],
            pltpu.SemaphoreType.DMA((k, team)),
            pltpu.SemaphoreType.DMA((k, team)),
            pltpu.SemaphoreType.DMA((k, n)),
            pltpu.SemaphoreType.DMA((k, n)),
            pltpu.SemaphoreType.DMA((k,)),
        ],
        compiler_params=pltpu.CompilerParams(
            collective_id=0, has_side_effects=True, vmem_limit_bytes=56 << 20
        ),
    )(
        pair.reshape(spots, chans), in_gain[None], in_bias[None], w_in, w_gate,
        out_gain[None], out_bias[None], w_out,
    )
    return update.reshape(rows, cols, w_out.shape[1])


def solution(mesh):
    n_ri, n_rj = mesh.shape["ri"], mesh.shape["rj"]
    return jax.shard_map(
        lambda *args: local(n_ri, n_rj, *args),
        mesh=mesh,
        in_specs=(P("ri", "rj", None), P(), P(), P(), P(), P(), P(), P()),
        out_specs=P("ri", "rj", None),
        check_vma=False,
    )
```

```python
import functools

import jax
import jax.numpy as jnp
from jax import lax
from jax.experimental import pallas as pl
from jax.experimental.pallas import tpu as pltpu
from jax.sharding import PartitionSpec as P

MESH = pl.DeviceIdType.MESH
LANES = 128
STEPS = 5


def plan(n_ri, n_rj, hidden):
    team = n_ri * n_rj // 2
    per = hidden // team
    if per == 8 and n_ri % 4 == 0:
        sizes = [(2, False), (2, False), (4, False)]
    elif per > 1:
        sizes = [(per // 2, False)] * 2
    else:
        sizes = [(per, False)]
    parts, base = [], 0
    for own, inner in sizes:
        owners = team // 2 if inner else team
        parts.append((own, base, owners, inner))
        base += own * owners
    return parts


def shifted(vregs, start):
    at, by = divmod(start, LANES)
    if by == 0:
        return vregs[at]
    return pltpu.roll(vregs[at], LANES - by, 1)


def body(n_ri, n_rj, rows, cols, parts, *refs):
    np_ = len(parts)
    fetched, kept = refs[:5], refs[5:8]
    tri_s, gate_s, *held = refs[8:13]
    pair, gain, bias, w_in, w_gate = refs[13:18]
    flat_s, ab_s, g_s, b_s, o_s, in_sem = refs[18:24]
    x_s, recv_s, t_s, got_s = (refs[24 + i * np_ : 24 + (i + 1) * np_] for i in range(4))
    send1, recv1, send2, recv2, loc = refs[24 + 4 * np_ :]

    n = n_ri * n_rj
    spots = rows * cols
    side = n_ri // 2
    team = n // 2
    depth = side * rows
    hidden = tri_s.shape[0]
    halves = cols // rows
    ri, rj = lax.axis_index("ri"), lax.axis_index("rj")
    me = ri * n_rj + rj
    seat = lax.rem(ri, side) * n_rj + rj
    base = (ri // side) * side
    half = ri // side
    low = jnp.where(half == 0, side // 2, 0)
    inner_seat = seat - low * n_rj
    is_inner = jnp.logical_and(inner_seat >= 0, inner_seat < team // 2)

    def other(d):
        return lax.rem(me + d, n)

    fetches = [
        pltpu.make_async_copy(src, dst, in_sem.at[i])
        for i, (src, dst) in enumerate(
            zip((*fetched, *kept), (pair, gain, bias, w_in, w_gate, *held))
        )
    ]
    for fetch in fetches:
        fetch.start()

    barrier = pltpu.get_barrier_semaphore()
    pl.semaphore_signal(
        barrier, inc=1, device_id=(lax.rem(ri + side, n_ri), rj), device_id_type=MESH
    )

    def greet(d, _):
        to = lax.rem(seat + team - d, team)
        pl.semaphore_signal(
            barrier, inc=1, device_id=(base + to // n_rj, lax.rem(to, n_rj)), device_id_type=MESH
        )
        return _

    lax.fori_loop(1, team, greet, 0)

    for fetch in fetches:
        fetch.wait()
    wt = w_in[...].T
    step = spots // STEPS

    def norm_in(i, _):
        at = pl.multiple_of(i * step, LANES)
        x = pair[pl.ds(at, step), :].astype(jnp.float32)
        mean = jnp.mean(x, axis=-1, keepdims=True)
        centered = x - mean
        var = jnp.mean(centered * centered, axis=-1, keepdims=True)
        flat = (centered * lax.rsqrt(var + 1e-05) * gain[...] + bias[...]).astype(jnp.bfloat16)
        flat_s[pl.ds(at, step), :] = flat
        return _

    lax.fori_loop(0, STEPS, norm_in, 0)

    def owner_of(t, e):
        if parts[t][3]:
            return base + low + e // n_rj, lax.rem(e, n_rj)
        return base + e // n_rj, lax.rem(e, n_rj)

    def owner_seat(t):
        return inner_seat if parts[t][3] else seat

    def owns(t, f):
        if parts[t][3]:
            pl.when(is_inner)(f)
        else:
            f()

    def copy_in(t, e, src):
        return pltpu.make_async_remote_copy(
            src_ref=x_s[t].at[e], dst_ref=recv_s[t].at[src], send_sem=send1.at[t, e],
            recv_sem=recv1.at[t, src], device_id=owner_of(t, e), device_id_type=MESH,
        )

    def copy_back(t, d, src):
        return pltpu.make_async_remote_copy(
            src_ref=t_s[t].at[d], dst_ref=got_s[t].at[src], send_sem=send2.at[t, d],
            recv_sem=recv2.at[t, src], device_id=(d // n_rj, lax.rem(d, n_rj)),
            device_id_type=MESH,
        )

    def slot(t, h, e):
        return h * parts[t][2] + e

    def my_slot(t):
        return slot(t, half, owner_seat(t))

    def project(t):
        own, first, owners, _ = parts[t]
        wide = own * owners
        each = 8 // own
        w = jnp.concatenate(
            [wt[g * hidden + first : g * hidden + first + wide] for g in range(4)], axis=0
        )

        def one(i, _):
            at = pl.multiple_of(i * step, LANES)
            proj = lax.dot_general(
                w, flat_s[pl.ds(at, step), :], (((1,), (1,)), ((), ())),
                preferred_element_type=jnp.float32,
            )
            ab_s[0, :wide, pl.ds(at, step)] = jax.nn.sigmoid(proj[wide : 2 * wide]) * proj[:wide]
            ab_s[1, :wide, pl.ds(at, step)] = (
                jax.nn.sigmoid(proj[3 * wide :]) * proj[2 * wide : 3 * wide]
            )
            return _

        lax.fori_loop(0, STEPS, one, 0)

        def split(p, _):
            at = pl.multiple_of(p * 8, 8)
            a8, b8 = ab_s[0, pl.ds(at, 8), :], ab_s[1, pl.ds(at, 8), :]
            for e in range(each):
                pick = slice(e * own, (e + 1) * own)
                x_s[t][p * each + e] = jnp.concatenate([a8[pick], b8[pick]], axis=0).astype(
                    jnp.bfloat16
                )
            return _

        lax.fori_loop(0, wide // 8, split, 0)

    def others(t, f):
        owners, mine = parts[t][2], owner_seat(t)

        def one(d, _):
            e = lax.rem(seat + d, owners)

            @pl.when(e != mine)
            def go():
                f(e)

            return _

        lax.fori_loop(0, owners, one, 0)

    for t in range(np_):
        project(t)
        if t == 0:
            pl.semaphore_wait(barrier, team)
        others(t, lambda e, t=t: copy_in(t, e, seat).start())

    def gates(i, _):
        at = pl.multiple_of(i * step, LANES)
        gate_s[pl.ds(at, step), :] = jax.nn.sigmoid(
            jnp.dot(flat_s[pl.ds(at, step), :], w_gate[...], preferred_element_type=jnp.float32)
        ).astype(jnp.bfloat16)
        return _

    lax.fori_loop(0, STEPS, gates, 0)

    def work(t):
        own = parts[t][0]
        lane = lax.broadcasted_iota(jnp.int32, (2 * own, LANES), 1)
        lane_o = lax.broadcasted_iota(jnp.int32, (own, LANES), 1)

        def unpack(block, src):
            i0 = (src // n_rj) * rows
            j = lax.rem(src, n_rj)
            wide = block.astype(jnp.float32)
            vregs = [wide[:, v * LANES : (v + 1) * LANES] for v in range(spots // LANES)]
            for k in range(rows):
                start = k * cols
                val = shifted(vregs, start)
                have = LANES - start % LANES
                if have < cols:
                    val = jnp.where(
                        lane < have, val, pltpu.roll(vregs[start // LANES + 1], have, 1)
                    )
                g_s[j, pl.ds(i0 + k, 2 * own, stride=depth), :] = val

        unpack(x_s[t][owner_seat(t)], seat)

        def take(d, _):
            src = lax.rem(seat + team - d, team)
            copy_in(t, 0, src).wait_recv()
            unpack(recv_s[t][src], src)
            return _

        lax.fori_loop(1, team, take, 0)

        for c in range(own):
            for q in range(n_rj):
                b_s[c, :, q * LANES : (q + 1) * LANES] = g_s[
                    q, (own + c) * depth : (own + c + 1) * depth, :
                ].astype(jnp.bfloat16)

        def emit(pp, _):
            p = lax.rem(pp + n_rj // 2 + ri // halves, n_rj)
            for c in range(own):
                lhs = g_s[p, c * depth : (c + 1) * depth, :].astype(jnp.bfloat16)
                product = lax.dot_general(
                    lhs, b_s[c], (((0,), (0,)), ((), ())), preferred_element_type=jnp.float32
                )
                for q in range(n_rj):
                    o_s[q, c * LANES : (c + 1) * LANES, :] = product[:, q * LANES : (q + 1) * LANES]

            def deliver(s, _):
                h, q = s // n_rj, lax.rem(s + rj, n_rj)
                d = (p * halves + h) * n_rj + q
                got = [
                    o_s[q, pl.ds(h * rows + r, own, stride=LANES), :] for r in range(rows)
                ]
                pieces = []
                for v in range(spots // LANES):
                    piece = None
                    for r in range(
                        (v * LANES) // cols, min(rows, ((v + 1) * LANES - 1) // cols + 1)
                    ):
                        at = r * cols - v * LANES
                        val = pltpu.roll(got[r], at % LANES, 1) if at % LANES else got[r]
                        piece = val if piece is None else jnp.where(lane_o >= at, val, piece)
                    pieces.append(piece)
                t_s[t][d] = jnp.concatenate(pieces, axis=1).astype(jnp.bfloat16)

                @pl.when(d != me)
                def start():
                    copy_back(t, d, my_slot(t)).start()

                return _

            lax.fori_loop(0, halves * n_rj, deliver, 0)
            return _

        lax.fori_loop(0, n_rj, emit, 0)
        pltpu.make_async_copy(t_s[t].at[me], got_s[t].at[my_slot(t)], loc.at[t]).start()

    for t in range(np_):
        owns(t, lambda t=t: work(t))

    for t in range(np_):
        own, first, owners, inner = parts[t]
        each = 8 // own
        others(t, lambda e, t=t: copy_in(t, e, seat).wait_send())

        def drain(t=t):
            def sent(d, _):
                copy_back(t, other(d), my_slot(t)).wait_send()
                return _

            lax.fori_loop(1, n, sent, 0)
            pltpu.make_async_copy(t_s[t].at[me], got_s[t].at[my_slot(t)], loc.at[t]).wait()

        owns(t, drain)
        mine = my_slot(t)
        owned = is_inner if inner else None

        def arrive(s, _, t=t):
            go = s != mine if owned is None else jnp.logical_or(s != mine, jnp.logical_not(owned))

            @pl.when(go)
            def wait():
                copy_back(t, 0, s).wait_recv()

            return _

        lax.fori_loop(0, 2 * owners, arrive, 0)

        def merge(p, _, t=t):
            at = pl.multiple_of(first + p * 8, 8)
            sums = [
                got_s[t][p * each + e].astype(jnp.float32)
                + got_s[t][owners + p * each + e].astype(jnp.float32)
                for e in range(each)
            ]
            tri_s[pl.ds(at, 8), :] = jnp.concatenate(sums, axis=0)
            return _

        lax.fori_loop(0, own * owners // 8, merge, 0)


def finish(tri, gate, out_gain, out_bias, w_out, upd, chunk_s, sem):
    hidden, spots = tri.shape
    step = spots // STEPS

    def column(row):
        tall = jnp.broadcast_to(row[...], (LANES, hidden)).T
        return jnp.concatenate([tall] * (step // LANES), axis=1)

    post_gain, post_bias = column(out_gain), column(out_bias)

    def put(i):
        return pltpu.make_async_copy(
            chunk_s.at[i], upd.at[pl.ds(pl.multiple_of(i * step, LANES), step), :], sem.at[i]
        )

    def one(i, _):
        at = pl.multiple_of(i * step, LANES)
        x = tri[:, pl.ds(at, step)]
        mean = jnp.mean(x, axis=0, keepdims=True)
        centered = x - mean
        var = jnp.mean(centered * centered, axis=0, keepdims=True)
        normed = (centered * lax.rsqrt(var + 1e-05) * post_gain + post_bias).astype(jnp.bfloat16)
        mixed = lax.dot_general(
            normed, w_out[...], (((0,), (0,)), ((), ())), preferred_element_type=jnp.float32
        )
        chunk_s[i] = (gate[pl.ds(at, step), :].astype(jnp.float32) * mixed).astype(jnp.bfloat16)
        put(i).start()
        return _

    lax.fori_loop(0, STEPS, one, 0)

    def done(i, _):
        put(i).wait()
        return _

    lax.fori_loop(0, STEPS, done, 0)


def local(n_ri, n_rj, pair, in_gain, in_bias, w_in, w_gate, out_gain, out_bias, w_out):
    rows, cols, chans = pair.shape
    hidden = w_out.shape[0]
    n = n_ri * n_rj
    team = n // 2
    spots = rows * cols
    depth = (n_ri // 2) * rows
    parts = plan(n_ri, n_rj, hidden)
    most = max(own for own, *_ in parts)
    wide = max(own * owners for own, _, owners, _ in parts)
    vmem = pl.BlockSpec(memory_space=pltpu.VMEM)
    bf16, f32 = jnp.bfloat16, jnp.float32
    k = len(parts)
    pre = (pair.reshape(spots, chans), in_gain[None], in_bias[None], w_in, w_gate)
    post = (out_gain[None], out_bias[None], w_out)
    tri, gate, *held = pl.pallas_call(
        functools.partial(body, n_ri, n_rj, rows, cols, parts),
        out_shape=(
            pltpu.VMEM((hidden, spots), f32),
            pltpu.VMEM((spots, chans), bf16),
            *[pltpu.VMEM(x.shape, x.dtype) for x in post],
        ),
        in_specs=[pl.BlockSpec(memory_space=pl.ANY)] * 8,
        out_specs=[vmem] * 5,
        scratch_shapes=[
            *[pltpu.VMEM(x.shape, x.dtype) for x in pre],
            pltpu.VMEM((spots, chans), bf16),
            pltpu.VMEM((2, wide, spots), f32),
            pltpu.VMEM((n_rj, 2 * most * depth, LANES), f32),
            pltpu.VMEM((most, depth, n_rj * LANES), bf16),
            pltpu.VMEM((n_rj, most * LANES, LANES), f32),
            pltpu.SemaphoreType.DMA((8,)),
            *[pltpu.VMEM((owners, 2 * own, spots), bf16) for own, _, owners, _ in parts],
            *[pltpu.VMEM((team, 2 * own, spots), bf16) for own, _, owners, _ in parts],
            *[pltpu.VMEM((n, own, spots), bf16) for own, _, owners, _ in parts],
            *[pltpu.VMEM((2 * owners, own, spots), bf16) for own, _, owners, _ in parts],
            pltpu.SemaphoreType.DMA((k, team)),
            pltpu.SemaphoreType.DMA((k, team)),
            pltpu.SemaphoreType.DMA((k, n)),
            pltpu.SemaphoreType.DMA((k, n)),
            pltpu.SemaphoreType.DMA((k,)),
        ],
        compiler_params=pltpu.CompilerParams(
            collective_id=0, has_side_effects=True, vmem_limit_bytes=40 << 20
        ),
    )(
        *[pltpu.with_memory_space_constraint(x, pltpu.HBM) for x in (*pre, *post)]
    )
    update = pl.pallas_call(
        finish,
        out_shape=jax.ShapeDtypeStruct((spots, w_out.shape[1]), bf16),
        in_specs=[vmem] * 5,
        out_specs=pl.BlockSpec(memory_space=pl.ANY),
        scratch_shapes=[
            pltpu.VMEM((STEPS, spots // STEPS, w_out.shape[1]), bf16),
            pltpu.SemaphoreType.DMA((STEPS,)),
        ],
        compiler_params=pltpu.CompilerParams(vmem_limit_bytes=12 << 20),
    )(
        pltpu.with_memory_space_constraint(tri, pltpu.VMEM),
        pltpu.with_memory_space_constraint(gate, pltpu.VMEM),
        *[pltpu.with_memory_space_constraint(x, pltpu.VMEM) for x in held],
    )
    return update.reshape(rows, cols, w_out.shape[1])


def solution(mesh):
    n_ri, n_rj = mesh.shape["ri"], mesh.shape["rj"]
    return jax.shard_map(
        lambda *args: local(n_ri, n_rj, *args),
        mesh=mesh,
        in_specs=(P("ri", "rj", None), P(), P(), P(), P(), P(), P(), P()),
        out_specs=P("ri", "rj", None),
        check_vma=False,
    )
```

```python
import functools

import jax
import jax.numpy as jnp
from jax import lax
from jax.experimental import pallas as pl
from jax.experimental.pallas import tpu as pltpu
from jax.sharding import PartitionSpec as P

MESH = pl.DeviceIdType.MESH
LANES = 128
STEPS = 5
NORM_STEPS = 5
END_STEPS = 5
LAG = 2
AHEAD = 8


def plan(n_ri, n_rj, hidden):
    side = n_ri // 2
    per = hidden // (side * n_rj)
    if per == 8 and n_ri % 4 == 0:
        sizes = [(2, False, False), (2, False, True), (4, False, True)]
    elif per > 1:
        sizes = [(per // 2, False, True)] * 2
    else:
        sizes = [(per, False, True)]
    parts, first = [], 0
    for own, inner, direct in sizes:
        oc = side // 2 if inner else side
        parts.append((own, first, oc, inner, direct))
        first += own * oc * n_rj
    return parts


def shifted(vregs, start):
    at, by = divmod(start, LANES)
    if by == 0:
        return vregs[at]
    return pltpu.roll(vregs[at], LANES - by, 1)


def body(n_ri, n_rj, rows, cols, parts, *refs):
    np_ = len(parts)
    fetched, kept = refs[:5], refs[5:8]
    gate_s, *held = refs[8:12]
    fin_s = refs[12 : 12 + np_]
    pair, gain, bias, w_in, w_gate, flat_s, ab_s, sum_s, g_s, b_s, o_s, in_sem = refs[
        12 + np_ : 24 + np_
    ]
    x_s, recv_s, t_s, got_s, fwd_s = (
        refs[24 + (i + 1) * np_ : 24 + (i + 2) * np_] for i in range(5)
    )
    send1, recv1, send2, recv2, send3, recv3 = refs[24 + 6 * np_ :]

    spots = rows * cols
    side = n_ri // 2
    team = side * n_rj
    depth = side * rows
    hidden = w_in.shape[1] // 4
    halves = cols // rows
    ri, rj = lax.axis_index("ri"), lax.axis_index("rj")
    half = ri // side
    base = half * side
    seat = (ri - base) * n_rj + rj
    me = ri * n_rj + rj
    n = n_ri * n_rj
    low = jnp.where(half == 0, side // 2, 0)
    is_inner = jnp.logical_and(ri - base >= low, ri - base < low + side // 2)
    vregs_n = spots // LANES

    fetches = [
        pltpu.make_async_copy(src, dst, in_sem.at[i])
        for i, (src, dst) in enumerate(
            zip((*fetched, *kept), (pair, gain, bias, w_in, w_gate, *held))
        )
    ]
    for fetch in fetches:
        fetch.start()

    barrier = pltpu.get_barrier_semaphore()
    pl.semaphore_signal(
        barrier, inc=1, device_id=(lax.rem(ri + side, n_ri), rj), device_id_type=MESH
    )

    def greet(d, _):
        to = lax.rem(seat + team - d, team)
        pl.semaphore_signal(
            barrier, inc=1, device_id=(base + to // n_rj, lax.rem(to, n_rj)), device_id_type=MESH
        )
        return _

    lax.fori_loop(1, team, greet, 0)

    for fetch in fetches:
        fetch.wait()
    wt = w_in[...].T
    step = spots // STEPS

    fine = spots // NORM_STEPS

    def norm_in(i, _):
        at = pl.multiple_of(i * fine, LANES)
        x = pair[pl.ds(at, fine), :].astype(jnp.float32)
        mean = jnp.mean(x, axis=-1, keepdims=True)
        centered = x - mean
        var = jnp.mean(centered * centered, axis=-1, keepdims=True)
        flat = (centered * lax.rsqrt(var + 1e-05) * gain[...] + bias[...]).astype(jnp.bfloat16)
        flat_s[pl.ds(at, fine), :] = flat
        return _

    lax.fori_loop(0, NORM_STEPS, norm_in, 0, unroll=5)

    def plane(t):
        return base + low if parts[t][3] else base

    def owner_seat(t):
        return (ri - plane(t)) * n_rj + rj

    def owns(t, f):
        if parts[t][3]:
            pl.when(is_inner)(f)
        else:
            f()

    def copy_in(t, e, src):
        return pltpu.make_async_remote_copy(
            src_ref=x_s[t].at[e], dst_ref=recv_s[t].at[src], send_sem=send1.at[t, e],
            recv_sem=recv1.at[t, src], device_id=(plane(t) + e // n_rj, lax.rem(e, n_rj)),
            device_id_type=MESH,
        )

    def keep_in(t):
        return pltpu.make_async_copy(
            x_s[t].at[owner_seat(t)], recv_s[t].at[seat], send1.at[t, owner_seat(t)]
        )

    def my_slot(t):
        return half * parts[t][2] + ri - plane(t)

    def copy_z(t, d, slot):
        return pltpu.make_async_remote_copy(
            src_ref=t_s[t].at[d], dst_ref=got_s[t].at[slot], send_sem=send2.at[t, d],
            recv_sem=recv2.at[t, slot], device_id=(d, rj), device_id_type=MESH,
        )

    def keep_z(t):
        return pltpu.make_async_copy(t_s[t].at[ri], got_s[t].at[my_slot(t)], send2.at[t, ri])

    def copy_all(t, d, slot):
        return pltpu.make_async_remote_copy(
            src_ref=t_s[t].at[d], dst_ref=got_s[t].at[slot], send_sem=send2.at[t, d],
            recv_sem=recv2.at[t, slot], device_id=(d // n_rj, lax.rem(d, n_rj)),
            device_id_type=MESH,
        )

    def all_slot(t):
        return half * parts[t][2] * n_rj + owner_seat(t)

    def keep_all(t):
        return pltpu.make_async_copy(t_s[t].at[me], got_s[t].at[all_slot(t)], send2.at[t, me])

    def copy_xy(t, q, src):
        return pltpu.make_async_remote_copy(
            src_ref=fwd_s[t].at[q], dst_ref=fin_s[t].at[src], send_sem=send3.at[t, q],
            recv_sem=recv3.at[t, src], device_id=(ri, q), device_id_type=MESH,
        )

    def keep_xy(t):
        return pltpu.make_async_copy(fwd_s[t].at[rj], fin_s[t].at[rj], send3.at[t, rj])

    def project(t):
        own, first, oc, *_ = parts[t]
        wide = own * oc * n_rj
        each = 8 // own
        w = jnp.concatenate(
            [wt[g * hidden + first : g * hidden + first + wide] for g in range(4)], axis=0
        )

        def one(i, _):
            at = pl.multiple_of(i * step, LANES)
            proj = lax.dot_general(
                w, flat_s[pl.ds(at, step), :], (((1,), (1,)), ((), ())),
                preferred_element_type=jnp.float32,
            )
            ab_s[0, :wide, pl.ds(at, step)] = jax.nn.sigmoid(proj[wide : 2 * wide]) * proj[:wide]
            ab_s[1, :wide, pl.ds(at, step)] = (
                jax.nn.sigmoid(proj[3 * wide :]) * proj[2 * wide : 3 * wide]
            )
            return _

        lax.fori_loop(0, STEPS, one, 0, unroll=5)

        def split(p, _):
            at = pl.multiple_of(p * 8, 8)
            a8, b8 = ab_s[0, pl.ds(at, 8), :], ab_s[1, pl.ds(at, 8), :]
            for k in range(each):
                pick = slice(k * own, (k + 1) * own)
                turn = p * each + k
                x_s[t][lax.rem(turn, oc) * n_rj + turn // oc] = jnp.concatenate(
                    [a8[pick], b8[pick]], axis=0
                ).astype(jnp.bfloat16)
            return _

        lax.fori_loop(0, wide // 8, split, 0)

    def others(t, f):
        owners, mine = parts[t][2] * n_rj, owner_seat(t)

        def one(d, _):
            e = lax.rem(seat + d, owners)

            @pl.when(e != mine)
            def go():
                f(e)

            return _

        lax.fori_loop(0, owners, one, 0)

    def publish(t):
        project(t)
        if t == 0:
            pl.semaphore_wait(barrier, team)
        others(t, lambda e: copy_in(t, e, seat).start())
        owns(t, lambda: keep_in(t).start())

    for t in range(min(AHEAD, np_)):
        publish(t)

    def gates(i, _):
        at = pl.multiple_of(i * step, LANES)
        gate_s[pl.ds(at, step), :] = jax.nn.sigmoid(
            jnp.dot(flat_s[pl.ds(at, step), :], w_gate[...], preferred_element_type=jnp.float32)
        ).astype(jnp.bfloat16)
        return _

    lax.fori_loop(0, STEPS, gates, 0)

    lane8 = lax.broadcasted_iota(jnp.int32, (8, LANES), 1)

    def work(t):
        own, direct = parts[t][0], parts[t][4]
        merge = 4 // own
        deep = depth // merge
        ranks = side // merge

        def take(turn, _):
            at = lax.rem(seat + team - turn, ranks * n_rj)
            r, j = at // n_rj, lax.rem(at, n_rj)
            for b in range(merge):
                src = (r + b * ranks) * n_rj + j

                @pl.when(src == seat)
                def kept():
                    keep_in(t).wait()

                @pl.when(src != seat)
                def came():
                    copy_in(t, 0, src).wait_recv()

            blocks = [
                recv_s[t][(r + b * ranks) * n_rj + j].astype(jnp.float32) for b in range(merge)
            ]
            wide = jnp.concatenate(blocks, axis=0) if merge > 1 else blocks[0]
            vregs = [wide[:, v * LANES : (v + 1) * LANES] for v in range(vregs_n)]
            for k in range(rows):
                start = k * cols
                val = shifted(vregs, start)
                have = LANES - start % LANES
                if have < cols:
                    val = jnp.where(
                        lane8 < have, val, pltpu.roll(vregs[start // LANES + 1], have, 1)
                    )
                g_s[j, pl.ds(r * rows + k, 8, stride=deep), :] = val
            return _

        lax.fori_loop(0, ranks * n_rj, take, 0)

        def operand(j, s):
            return [
                g_s[j, (b * 2 * own + s) * deep : (b * 2 * own + s + 1) * deep, :].astype(
                    jnp.bfloat16
                )
                for b in range(merge)
            ]

        for c in range(own):
            for q in range(n_rj):
                b_s[c, :, q * LANES : (q + 1) * LANES] = jnp.concatenate(
                    operand(q, own + c), axis=0
                )

        def emit(pp, _):
            p = lax.rem(pp + (1 - half) * (n_rj // 2), n_rj)
            for c in range(own):
                product = lax.dot_general(
                    jnp.concatenate(operand(p, c), axis=0), b_s[c], (((0,), (0,)), ((), ())),
                    preferred_element_type=jnp.float32,
                )
                for q in range(n_rj):
                    if direct:
                        at = lax.rem(q + n_rj - rj, n_rj) * own + c
                    else:
                        at = c * n_rj + q
                    o_s[pl.ds(pl.multiple_of(at * LANES, LANES), LANES), :] = product[
                        :, q * LANES : (q + 1) * LANES
                    ]

            def deliver(h, _):
                d = p * halves + h
                slabs = []
                for g in range(own * n_rj // 8):
                    got = [
                        o_s[pl.ds(g * 8 * LANES + h * rows + r, 8, stride=LANES), :]
                        for r in range(rows)
                    ]
                    pieces = []
                    for v in range(vregs_n):
                        piece = None
                        for r in range(
                            (v * LANES) // cols, min(rows, ((v + 1) * LANES - 1) // cols + 1)
                        ):
                            at = r * cols - v * LANES
                            val = pltpu.roll(got[r], at % LANES, 1) if at % LANES else got[r]
                            piece = val if piece is None else jnp.where(lane8 >= at, val, piece)
                        pieces.append(piece)
                    slabs.append(jnp.concatenate(pieces, axis=1))
                if direct:
                    for turn in range(n_rj):
                        to = d * n_rj + lax.rem(turn + rj, n_rj)
                        at = turn * own
                        t_s[t][to] = slabs[at // 8][at % 8 : at % 8 + own].astype(jnp.bfloat16)

                        @pl.when(to != me)
                        def go(to=to):
                            copy_all(t, to, all_slot(t)).start()

                    return _

                slab = jnp.concatenate(slabs, axis=0) if len(slabs) > 1 else slabs[0]
                t_s[t][d] = slab.astype(jnp.bfloat16)

                @pl.when(d != ri)
                def start():
                    copy_z(t, d, my_slot(t)).start()

                return _

            lax.fori_loop(0, halves, deliver, 0)
            return _

        lax.fori_loop(0, n_rj, emit, 0)
        (keep_all if direct else keep_z)(t).start()

    def total(t):
        own, first, oc, inner, _ = parts[t]
        mine = my_slot(t)

        def arrive(s, _):
            go = s != mine
            if inner:
                go = jnp.logical_or(go, jnp.logical_not(is_inner))

            @pl.when(go)
            def wait():
                copy_z(t, 0, s).wait_recv()

            return _

        lax.fori_loop(0, 2 * oc, arrive, 0)
        owns(t, lambda: keep_z(t).wait())
        tall = own * n_rj

        def add(o, _):
            both = got_s[t][o].astype(jnp.float32) + got_s[t][oc + o].astype(jnp.float32)
            at = pl.multiple_of(o * tall, 8)
            for v in range(vregs_n):
                sum_s[v, pl.ds(at, tall), :] = both[:, v * LANES : (v + 1) * LANES]
            return _

        lax.fori_loop(0, oc, add, 0)

        def forward(d, _):
            q = lax.rem(rj + 1 + d, n_rj)
            fwd_s[t][q] = jnp.concatenate(
                [sum_s[v, pl.ds(q, oc * own, stride=n_rj), :] for v in range(vregs_n)], axis=1
            ).astype(jnp.bfloat16)

            @pl.when(q != rj)
            def start():
                copy_xy(t, q, rj).start()

            return _

        lax.fori_loop(0, n_rj, forward, 0)
        keep_xy(t).start()

    for t in range(np_):
        owns(t, lambda t=t: work(t))
        if t + AHEAD < np_:
            publish(t + AHEAD)
        if t >= LAG and not parts[t - LAG][4]:
            total(t - LAG)
    for t in range(max(np_ - LAG, 0), np_):
        if not parts[t][4]:
            total(t)

    def settle(t):
        def drain():
            def sent(d, _):
                @pl.when(d != ri)
                def wait():
                    copy_z(t, d, my_slot(t)).wait_send()

                return _

            lax.fori_loop(0, n_ri, sent, 0)

        owns(t, drain)

        def last(d, _):
            q = lax.rem(rj + d, n_rj)
            copy_xy(t, q, rj).wait_send()
            copy_xy(t, 0, q).wait_recv()
            return _

        lax.fori_loop(1, n_rj, last, 0)
        keep_xy(t).wait()

    def gather(t):
        own, first, oc, inner, _ = parts[t]
        owners, mine, each = oc * n_rj, all_slot(t), 8 // own

        def drain():
            def sent(d, _):
                copy_all(t, lax.rem(me + d, n), mine).wait_send()
                return _

            lax.fori_loop(1, n, sent, 0)
            keep_all(t).wait()

        owns(t, drain)

        def arrive(s):
            go = s != mine
            if inner:
                go = jnp.logical_or(go, jnp.logical_not(is_inner))

            @pl.when(go)
            def wait():
                copy_all(t, 0, s).wait_recv()

        def merge(p, _):
            sums = []
            for k in range(each):
                turn = p * each + k
                e = lax.rem(turn, oc) * n_rj + turn // oc
                arrive(e)
                arrive(owners + e)
                sums.append(
                    got_s[t][e].astype(jnp.float32) + got_s[t][owners + e].astype(jnp.float32)
                )
            fin_s[t][0, pl.ds(pl.multiple_of(p * 8, 8), 8), :] = jnp.concatenate(sums, axis=0)
            return _

        lax.fori_loop(0, own * owners // 8, merge, 0)

    for t in range(np_):
        others(t, lambda e, t=t: copy_in(t, e, seat).wait_send())

        if parts[t][4]:
            gather(t)
        else:
            settle(t)


def finish(gate, out_gain, out_bias, w_out, *refs):
    *parts, upd, chunk_s, sem = refs
    hidden = w_out.shape[0]
    spots = gate.shape[0]
    step = spots // END_STEPS

    def column(row):
        tall = jnp.broadcast_to(row[...], (LANES, hidden)).T
        return jnp.concatenate([tall] * (step // LANES), axis=1)

    post_gain, post_bias = column(out_gain), column(out_bias)

    def put(i):
        return pltpu.make_async_copy(
            chunk_s.at[i], upd.at[pl.ds(pl.multiple_of(i * step, LANES), step), :], sem.at[i]
        )

    def one(i, _):
        at = pl.multiple_of(i * step, LANES)
        x = jnp.concatenate(
            [
                part[q, :, pl.ds(at, step)].astype(jnp.float32)
                for part in parts
                for q in range(part.shape[0])
            ],
            axis=0,
        )
        mean = jnp.mean(x, axis=0, keepdims=True)
        centered = x - mean
        var = jnp.mean(centered * centered, axis=0, keepdims=True)
        normed = (centered * lax.rsqrt(var + 1e-05) * post_gain + post_bias).astype(jnp.bfloat16)
        mixed = lax.dot_general(
            normed, w_out[...], (((0,), (0,)), ((), ())), preferred_element_type=jnp.float32
        )
        chunk_s[i] = (gate[pl.ds(at, step), :].astype(jnp.float32) * mixed).astype(jnp.bfloat16)
        put(i).start()
        return _

    lax.fori_loop(0, END_STEPS, one, 0, unroll=5)

    def done(i, _):
        put(i).wait()
        return _

    lax.fori_loop(0, END_STEPS, done, 0)


def local(n_ri, n_rj, pair, in_gain, in_bias, w_in, w_gate, out_gain, out_bias, w_out):
    rows, cols, chans = pair.shape
    hidden = w_out.shape[0]
    team = n_ri // 2 * n_rj
    spots = rows * cols
    depth = (n_ri // 2) * rows
    parts = plan(n_ri, n_rj, hidden)
    most = max(own for own, *_ in parts)
    col = max(own * oc for own, _, oc, *_ in parts)
    vmem = pl.BlockSpec(memory_space=pltpu.VMEM)
    bf16, f32 = jnp.bfloat16, jnp.float32
    k = len(parts)
    pre = (pair.reshape(spots, chans), in_gain[None], in_bias[None], w_in, w_gate)
    post = (out_gain[None], out_bias[None], w_out)
    fins = [
        ((1, n_rj * own * oc, spots), f32) if direct else ((n_rj, own * oc, spots), bf16)
        for own, _, oc, _, direct in parts
    ]
    n = n_ri * n_rj
    tiny = (1, 8, LANES)
    handed = pl.pallas_call(
        functools.partial(body, n_ri, n_rj, rows, cols, parts),
        out_shape=(
            pltpu.VMEM((spots, chans), bf16),
            *[pltpu.VMEM(x.shape, x.dtype) for x in post],
            *[pltpu.VMEM(*fin) for fin in fins],
        ),
        in_specs=[pl.BlockSpec(memory_space=pl.ANY)] * 8,
        out_specs=[vmem] * (4 + k),
        scratch_shapes=[
            *[pltpu.VMEM(x.shape, x.dtype) for x in pre],
            pltpu.VMEM((spots, chans), bf16),
            pltpu.VMEM((2, col * n_rj, spots), f32),
            pltpu.VMEM((spots // LANES, col * n_rj, LANES), f32),
            pltpu.VMEM((n_rj, 2 * most * depth, LANES), f32),
            pltpu.VMEM((most, depth, n_rj * LANES), bf16),
            pltpu.VMEM((most * n_rj * LANES, LANES), f32),
            pltpu.SemaphoreType.DMA((8,)),
            *[pltpu.VMEM((oc * n_rj, 2 * own, spots), bf16) for own, _, oc, *_ in parts],
            *[pltpu.VMEM((team, 2 * own, spots), bf16) for own, _, oc, *_ in parts],
            *[
                pltpu.VMEM((n, own, spots) if direct else (n_ri, own * n_rj, spots), bf16)
                for own, _, oc, _, direct in parts
            ],
            *[
                pltpu.VMEM(
                    (2 * oc * n_rj, own, spots) if direct else (2 * oc, own * n_rj, spots), bf16
                )
                for own, _, oc, _, direct in parts
            ],
            *[pltpu.VMEM(tiny if direct else fin[0], bf16) for fin, (*_, direct) in zip(fins, parts)],
            pltpu.SemaphoreType.DMA((k, team)),
            pltpu.SemaphoreType.DMA((k, team)),
            pltpu.SemaphoreType.DMA((k, n)),
            pltpu.SemaphoreType.DMA((k, n)),
            pltpu.SemaphoreType.DMA((k, n_rj)),
            pltpu.SemaphoreType.DMA((k, n_rj)),
        ],
        compiler_params=pltpu.CompilerParams(
            collective_id=0, has_side_effects=True, vmem_limit_bytes=40 << 20
        ),
    )(
        *[pltpu.with_memory_space_constraint(x, pltpu.HBM) for x in (*pre, *post)]
    )
    update = pl.pallas_call(
        finish,
        out_shape=jax.ShapeDtypeStruct((spots, w_out.shape[1]), bf16),
        in_specs=[vmem] * (4 + k),
        out_specs=pl.BlockSpec(memory_space=pl.ANY),
        scratch_shapes=[
            pltpu.VMEM((END_STEPS, spots // END_STEPS, w_out.shape[1]), bf16),
            pltpu.SemaphoreType.DMA((END_STEPS,)),
        ],
        compiler_params=pltpu.CompilerParams(vmem_limit_bytes=12 << 20),
    )(*[pltpu.with_memory_space_constraint(x, pltpu.VMEM) for x in handed])
    return update.reshape(rows, cols, w_out.shape[1])


def solution(mesh):
    n_ri, n_rj = mesh.shape["ri"], mesh.shape["rj"]
    return jax.shard_map(
        lambda *args: local(n_ri, n_rj, *args),
        mesh=mesh,
        in_specs=(P("ri", "rj", None), P(), P(), P(), P(), P(), P(), P()),
        out_specs=P("ri", "rj", None),
        check_vma=False,
    )
```

```python
import functools

import jax
import jax.numpy as jnp
from jax import lax
from jax.experimental import pallas as pl
from jax.experimental.pallas import tpu as pltpu
from jax.sharding import PartitionSpec as P

MESH = pl.DeviceIdType.MESH
LANES = 128
STEPS = 5
NORM_STEPS = 5
END_STEPS = 5
LAG = 2
AHEAD = 8


def plan(n_ri, n_rj, hidden):
    side = n_ri // 2
    per = hidden // (side * n_rj)
    if per == 8 and n_ri % 4 == 0:
        sizes = [(2, False, False), (2, False, True), (4, False, True)]
    elif per > 1:
        sizes = [(per // 2, False, True)] * 2
    else:
        sizes = [(per, False, True)]
    parts, first = [], 0
    for own, inner, direct in sizes:
        oc = side // 2 if inner else side
        parts.append((own, first, oc, inner, direct))
        first += own * oc * n_rj
    return parts


def shifted(vregs, start):
    at, by = divmod(start, LANES)
    if by == 0:
        return vregs[at]
    return pltpu.roll(vregs[at], LANES - by, 1)


def body(n_ri, n_rj, rows, cols, parts, *refs):
    np_ = len(parts)
    fetched, kept = refs[:5], refs[5:8]
    gate_s, *held = refs[8:12]
    fin_s = refs[12 : 12 + np_]
    pair, gain, bias, w_in, w_gate, flat_s, ab_s, sum_s, g_s, b_s, o_s, in_sem = refs[
        12 + np_ : 24 + np_
    ]
    x_s, recv_s, t_s, got_s, fwd_s = (
        refs[24 + (i + 1) * np_ : 24 + (i + 2) * np_] for i in range(5)
    )
    send1, recv1, send2, recv2, send3, recv3 = refs[24 + 6 * np_ :]

    spots = rows * cols
    side = n_ri // 2
    team = side * n_rj
    depth = side * rows
    hidden = w_in.shape[1] // 4
    halves = cols // rows
    ri, rj = lax.axis_index("ri"), lax.axis_index("rj")
    half = ri // side
    base = half * side
    seat = (ri - base) * n_rj + rj
    me = ri * n_rj + rj
    n = n_ri * n_rj
    low = jnp.where(half == 0, side // 2, 0)
    is_inner = jnp.logical_and(ri - base >= low, ri - base < low + side // 2)
    vregs_n = spots // LANES

    fetches = [
        pltpu.make_async_copy(src, dst, in_sem.at[i])
        for i, (src, dst) in enumerate(
            zip((*fetched, *kept), (pair, gain, bias, w_in, w_gate, *held))
        )
    ]
    for fetch in fetches:
        fetch.start()

    barrier = pltpu.get_barrier_semaphore()
    pl.semaphore_signal(
        barrier, inc=1, device_id=(lax.rem(ri + side, n_ri), rj), device_id_type=MESH
    )

    def greet(d, _):
        to = lax.rem(seat + team - d, team)
        pl.semaphore_signal(
            barrier, inc=1, device_id=(base + to // n_rj, lax.rem(to, n_rj)), device_id_type=MESH
        )
        return _

    lax.fori_loop(1, team, greet, 0)

    for fetch in fetches:
        fetch.wait()
    wt = w_in[...].T
    step = spots // STEPS

    fine = spots // NORM_STEPS

    def norm_in(i, _):
        at = pl.multiple_of(i * fine, LANES)
        x = pair[pl.ds(at, fine), :].astype(jnp.float32)
        mean = jnp.mean(x, axis=-1, keepdims=True)
        centered = x - mean
        var = jnp.mean(centered * centered, axis=-1, keepdims=True)
        flat = (centered * lax.rsqrt(var + 1e-05) * gain[...] + bias[...]).astype(jnp.bfloat16)
        flat_s[pl.ds(at, fine), :] = flat
        return _

    lax.fori_loop(0, NORM_STEPS, norm_in, 0, unroll=5)

    def plane(t):
        return base + low if parts[t][3] else base

    def owner_seat(t):
        return (ri - plane(t)) * n_rj + rj

    def owns(t, f):
        if parts[t][3]:
            pl.when(is_inner)(f)
        else:
            f()

    def copy_in(t, e, src):
        return pltpu.make_async_remote_copy(
            src_ref=x_s[t].at[e], dst_ref=recv_s[t].at[src], send_sem=send1.at[t, e],
            recv_sem=recv1.at[t, src], device_id=(plane(t) + e // n_rj, lax.rem(e, n_rj)),
            device_id_type=MESH,
        )

    def keep_in(t):
        return pltpu.make_async_copy(
            x_s[t].at[owner_seat(t)], recv_s[t].at[seat], send1.at[t, owner_seat(t)]
        )

    def my_slot(t):
        return half * parts[t][2] + ri - plane(t)

    def copy_z(t, d, slot):
        return pltpu.make_async_remote_copy(
            src_ref=t_s[t].at[d], dst_ref=got_s[t].at[slot], send_sem=send2.at[t, d],
            recv_sem=recv2.at[t, slot], device_id=(d, rj), device_id_type=MESH,
        )

    def keep_z(t):
        return pltpu.make_async_copy(t_s[t].at[ri], got_s[t].at[my_slot(t)], send2.at[t, ri])

    def copy_all(t, d, slot):
        return pltpu.make_async_remote_copy(
            src_ref=t_s[t].at[d], dst_ref=got_s[t].at[slot], send_sem=send2.at[t, d],
            recv_sem=recv2.at[t, slot], device_id=(d // n_rj, lax.rem(d, n_rj)),
            device_id_type=MESH,
        )

    def all_slot(t):
        return half * parts[t][2] * n_rj + owner_seat(t)

    def keep_all(t):
        return pltpu.make_async_copy(t_s[t].at[me], got_s[t].at[all_slot(t)], send2.at[t, me])

    def copy_xy(t, q, src):
        return pltpu.make_async_remote_copy(
            src_ref=fwd_s[t].at[q], dst_ref=fin_s[t].at[src], send_sem=send3.at[t, q],
            recv_sem=recv3.at[t, src], device_id=(ri, q), device_id_type=MESH,
        )

    def keep_xy(t):
        return pltpu.make_async_copy(fwd_s[t].at[rj], fin_s[t].at[rj], send3.at[t, rj])

    def project(t):
        own, first, oc, *_ = parts[t]
        wide = own * oc * n_rj
        each = 8 // own
        w = jnp.concatenate(
            [wt[g * hidden + first : g * hidden + first + wide] for g in range(4)], axis=0
        )

        def one(i, _):
            at = pl.multiple_of(i * step, LANES)
            proj = lax.dot_general(
                w, flat_s[pl.ds(at, step), :], (((1,), (1,)), ((), ())),
                preferred_element_type=jnp.float32,
            )
            ab_s[0, :wide, pl.ds(at, step)] = jax.nn.sigmoid(proj[wide : 2 * wide]) * proj[:wide]
            ab_s[1, :wide, pl.ds(at, step)] = (
                jax.nn.sigmoid(proj[3 * wide :]) * proj[2 * wide : 3 * wide]
            )
            return _

        lax.fori_loop(0, STEPS, one, 0, unroll=5)

        def split(p, _):
            at = pl.multiple_of(p * 8, 8)
            a8, b8 = ab_s[0, pl.ds(at, 8), :], ab_s[1, pl.ds(at, 8), :]
            for k in range(each):
                pick = slice(k * own, (k + 1) * own)
                turn = p * each + k
                x_s[t][lax.rem(turn, oc) * n_rj + turn // oc] = jnp.concatenate(
                    [a8[pick], b8[pick]], axis=0
                ).astype(jnp.bfloat16)
            return _

        lax.fori_loop(0, wide // 8, split, 0)

    def others(t, f):
        owners, mine = parts[t][2] * n_rj, owner_seat(t)

        def one(d, _):
            e = lax.rem((seat // (owners // 2) + 1 + d // (owners // 2)) * (owners // 2) + lax.rem(seat + d, owners // 2), owners)

            @pl.when(e != mine)
            def go():
                f(e)

            return _

        lax.fori_loop(0, owners, one, 0)

    def publish(t):
        project(t)
        if t == 0:
            pl.semaphore_wait(barrier, team)
        others(t, lambda e: copy_in(t, e, seat).start())
        owns(t, lambda: keep_in(t).start())

    for t in range(min(AHEAD, np_)):
        publish(t)

    def gates(i, _):
        at = pl.multiple_of(i * step, LANES)
        gate_s[pl.ds(at, step), :] = jax.nn.sigmoid(
            jnp.dot(flat_s[pl.ds(at, step), :], w_gate[...], preferred_element_type=jnp.float32)
        ).astype(jnp.bfloat16)
        return _

    lax.fori_loop(0, STEPS, gates, 0)

    lane8 = lax.broadcasted_iota(jnp.int32, (8, LANES), 1)

    def work(t):
        own, direct = parts[t][0], parts[t][4]
        merge = 4 // own
        deep = depth // merge
        ranks = side // merge

        def take(turn, _):
            lot = ranks * n_rj
            side_lot = team // 2
            if lot == team:
                at = lax.rem((seat // side_lot + 1 + turn // side_lot) * side_lot + lax.rem(seat + team - turn, side_lot), team)
            else:
                at = lax.rem(seat + team - turn, lot)
            r, j = at // n_rj, lax.rem(at, n_rj)
            for b in range(merge):
                src = (r + b * ranks) * n_rj + j

                @pl.when(src == seat)
                def kept():
                    keep_in(t).wait()

                @pl.when(src != seat)
                def came():
                    copy_in(t, 0, src).wait_recv()

            blocks = [
                recv_s[t][(r + b * ranks) * n_rj + j].astype(jnp.float32) for b in range(merge)
            ]
            wide = jnp.concatenate(blocks, axis=0) if merge > 1 else blocks[0]
            vregs = [wide[:, v * LANES : (v + 1) * LANES] for v in range(vregs_n)]
            for k in range(rows):
                start = k * cols
                val = shifted(vregs, start)
                have = LANES - start % LANES
                if have < cols:
                    val = jnp.where(
                        lane8 < have, val, pltpu.roll(vregs[start // LANES + 1], have, 1)
                    )
                g_s[j, pl.ds(r * rows + k, 8, stride=deep), :] = val
            return _

        lax.fori_loop(0, ranks * n_rj, take, 0)

        def operand(j, s):
            return [
                g_s[j, (b * 2 * own + s) * deep : (b * 2 * own + s + 1) * deep, :].astype(
                    jnp.bfloat16
                )
                for b in range(merge)
            ]

        for c in range(own):
            for q in range(n_rj):
                b_s[c, :, q * LANES : (q + 1) * LANES] = jnp.concatenate(
                    operand(q, own + c), axis=0
                )

        def emit(pp, _):
            p = lax.rem(pp + (1 - half) * (n_rj // 2), n_rj)
            for c in range(own):
                product = lax.dot_general(
                    jnp.concatenate(operand(p, c), axis=0), b_s[c], (((0,), (0,)), ((), ())),
                    preferred_element_type=jnp.float32,
                )
                for q in range(n_rj):
                    if direct:
                        at = lax.rem(q + n_rj - rj, n_rj) * own + c
                    else:
                        at = c * n_rj + q
                    o_s[pl.ds(pl.multiple_of(at * LANES, LANES), LANES), :] = product[
                        :, q * LANES : (q + 1) * LANES
                    ]

            def deliver(h, _):
                d = p * halves + h
                slabs = []
                for g in range(own * n_rj // 8):
                    got = [
                        o_s[pl.ds(g * 8 * LANES + h * rows + r, 8, stride=LANES), :]
                        for r in range(rows)
                    ]
                    pieces = []
                    for v in range(vregs_n):
                        piece = None
                        for r in range(
                            (v * LANES) // cols, min(rows, ((v + 1) * LANES - 1) // cols + 1)
                        ):
                            at = r * cols - v * LANES
                            val = pltpu.roll(got[r], at % LANES, 1) if at % LANES else got[r]
                            piece = val if piece is None else jnp.where(lane8 >= at, val, piece)
                        pieces.append(piece)
                    slabs.append(jnp.concatenate(pieces, axis=1))
                if direct:
                    for turn in range(n_rj):
                        to = d * n_rj + lax.rem(turn + rj, n_rj)
                        at = turn * own
                        t_s[t][to] = slabs[at // 8][at % 8 : at % 8 + own].astype(jnp.bfloat16)

                        @pl.when(to != me)
                        def go(to=to):
                            copy_all(t, to, all_slot(t)).start()

                    return _

                slab = jnp.concatenate(slabs, axis=0) if len(slabs) > 1 else slabs[0]
                t_s[t][d] = slab.astype(jnp.bfloat16)

                @pl.when(d != ri)
                def start():
                    copy_z(t, d, my_slot(t)).start()

                return _

            lax.fori_loop(0, halves, deliver, 0)
            return _

        lax.fori_loop(0, n_rj, emit, 0)
        (keep_all if direct else keep_z)(t).start()

    def total(t):
        own, first, oc, inner, _ = parts[t]
        mine = my_slot(t)

        def arrive(s, _):
            go = s != mine
            if inner:
                go = jnp.logical_or(go, jnp.logical_not(is_inner))

            @pl.when(go)
            def wait():
                copy_z(t, 0, s).wait_recv()

            return _

        lax.fori_loop(0, 2 * oc, arrive, 0)
        owns(t, lambda: keep_z(t).wait())
        tall = own * n_rj

        def add(o, _):
            both = got_s[t][o].astype(jnp.float32) + got_s[t][oc + o].astype(jnp.float32)
            at = pl.multiple_of(o * tall, 8)
            for v in range(vregs_n):
                sum_s[v, pl.ds(at, tall), :] = both[:, v * LANES : (v + 1) * LANES]
            return _

        lax.fori_loop(0, oc, add, 0)

        def forward(d, _):
            q = lax.rem(rj + 1 + d, n_rj)
            fwd_s[t][q] = jnp.concatenate(
                [sum_s[v, pl.ds(q, oc * own, stride=n_rj), :] for v in range(vregs_n)], axis=1
            ).astype(jnp.bfloat16)

            @pl.when(q != rj)
            def start():
                copy_xy(t, q, rj).start()

            return _

        lax.fori_loop(0, n_rj, forward, 0)
        keep_xy(t).start()

    for t in range(np_):
        owns(t, lambda t=t: work(t))
        if t + AHEAD < np_:
            publish(t + AHEAD)
        if t >= LAG and not parts[t - LAG][4]:
            total(t - LAG)
    for t in range(max(np_ - LAG, 0), np_):
        if not parts[t][4]:
            total(t)

    def settle(t):
        def drain():
            def sent(d, _):
                @pl.when(d != ri)
                def wait():
                    copy_z(t, d, my_slot(t)).wait_send()

                return _

            lax.fori_loop(0, n_ri, sent, 0)

        owns(t, drain)

        def last(d, _):
            q = lax.rem(rj + d, n_rj)
            copy_xy(t, q, rj).wait_send()
            copy_xy(t, 0, q).wait_recv()
            return _

        lax.fori_loop(1, n_rj, last, 0)
        keep_xy(t).wait()

    def gather(t):
        own, first, oc, inner, _ = parts[t]
        owners, mine, each = oc * n_rj, all_slot(t), 8 // own

        def drain():
            def sent(d, _):
                copy_all(t, lax.rem(me + d, n), mine).wait_send()
                return _

            lax.fori_loop(1, n, sent, 0)
            keep_all(t).wait()

        owns(t, drain)

        def arrive(s):
            go = s != mine
            if inner:
                go = jnp.logical_or(go, jnp.logical_not(is_inner))

            @pl.when(go)
            def wait():
                copy_all(t, 0, s).wait_recv()

        def merge(p, _):
            sums = []
            for k in range(each):
                turn = p * each + k
                e = lax.rem(turn, oc) * n_rj + turn // oc
                arrive(e)
                arrive(owners + e)
                sums.append(
                    got_s[t][e].astype(jnp.float32) + got_s[t][owners + e].astype(jnp.float32)
                )
            fin_s[t][0, pl.ds(pl.multiple_of(p * 8, 8), 8), :] = jnp.concatenate(sums, axis=0)
            return _

        lax.fori_loop(0, own * owners // 8, merge, 0)

    for t in range(np_):
        others(t, lambda e, t=t: copy_in(t, e, seat).wait_send())

        if parts[t][4]:
            gather(t)
        else:
            settle(t)


def finish(gate, out_gain, out_bias, w_out, *refs):
    *parts, upd, chunk_s, sem = refs
    hidden = w_out.shape[0]
    spots = gate.shape[0]
    step = spots // END_STEPS

    def column(row):
        tall = jnp.broadcast_to(row[...], (LANES, hidden)).T
        return jnp.concatenate([tall] * (step // LANES), axis=1)

    post_gain, post_bias = column(out_gain), column(out_bias)

    def put(i):
        return pltpu.make_async_copy(
            chunk_s.at[i], upd.at[pl.ds(pl.multiple_of(i * step, LANES), step), :], sem.at[i]
        )

    def one(i, _):
        at = pl.multiple_of(i * step, LANES)
        x = jnp.concatenate(
            [
                part[q, :, pl.ds(at, step)].astype(jnp.float32)
                for part in parts
                for q in range(part.shape[0])
            ],
            axis=0,
        )
        mean = jnp.mean(x, axis=0, keepdims=True)
        centered = x - mean
        var = jnp.mean(centered * centered, axis=0, keepdims=True)
        normed = (centered * lax.rsqrt(var + 1e-05) * post_gain + post_bias).astype(jnp.bfloat16)
        mixed = lax.dot_general(
            normed, w_out[...], (((0,), (0,)), ((), ())), preferred_element_type=jnp.float32
        )
        chunk_s[i] = (gate[pl.ds(at, step), :].astype(jnp.float32) * mixed).astype(jnp.bfloat16)
        put(i).start()
        return _

    lax.fori_loop(0, END_STEPS, one, 0, unroll=5)

    def done(i, _):
        put(i).wait()
        return _

    lax.fori_loop(0, END_STEPS, done, 0)


def local(n_ri, n_rj, pair, in_gain, in_bias, w_in, w_gate, out_gain, out_bias, w_out):
    rows, cols, chans = pair.shape
    hidden = w_out.shape[0]
    team = n_ri // 2 * n_rj
    spots = rows * cols
    depth = (n_ri // 2) * rows
    parts = plan(n_ri, n_rj, hidden)
    most = max(own for own, *_ in parts)
    col = max(own * oc for own, _, oc, *_ in parts)
    vmem = pl.BlockSpec(memory_space=pltpu.VMEM)
    bf16, f32 = jnp.bfloat16, jnp.float32
    k = len(parts)
    pre = (pair.reshape(spots, chans), in_gain[None], in_bias[None], w_in, w_gate)
    post = (out_gain[None], out_bias[None], w_out)
    fins = [
        ((1, n_rj * own * oc, spots), f32) if direct else ((n_rj, own * oc, spots), bf16)
        for own, _, oc, _, direct in parts
    ]
    n = n_ri * n_rj
    tiny = (1, 8, LANES)
    handed = pl.pallas_call(
        functools.partial(body, n_ri, n_rj, rows, cols, parts),
        out_shape=(
            pltpu.VMEM((spots, chans), bf16),
            *[pltpu.VMEM(x.shape, x.dtype) for x in post],
            *[pltpu.VMEM(*fin) for fin in fins],
        ),
        in_specs=[pl.BlockSpec(memory_space=pl.ANY)] * 8,
        out_specs=[vmem] * (4 + k),
        scratch_shapes=[
            *[pltpu.VMEM(x.shape, x.dtype) for x in pre],
            pltpu.VMEM((spots, chans), bf16),
            pltpu.VMEM((2, col * n_rj, spots), f32),
            pltpu.VMEM((spots // LANES, col * n_rj, LANES), f32),
            pltpu.VMEM((n_rj, 2 * most * depth, LANES), f32),
            pltpu.VMEM((most, depth, n_rj * LANES), bf16),
            pltpu.VMEM((most * n_rj * LANES, LANES), f32),
            pltpu.SemaphoreType.DMA((8,)),
            *[pltpu.VMEM((oc * n_rj, 2 * own, spots), bf16) for own, _, oc, *_ in parts],
            *[pltpu.VMEM((team, 2 * own, spots), bf16) for own, _, oc, *_ in parts],
            *[
                pltpu.VMEM((n, own, spots) if direct else (n_ri, own * n_rj, spots), bf16)
                for own, _, oc, _, direct in parts
            ],
            *[
                pltpu.VMEM(
                    (2 * oc * n_rj, own, spots) if direct else (2 * oc, own * n_rj, spots), bf16
                )
                for own, _, oc, _, direct in parts
            ],
            *[pltpu.VMEM(tiny if direct else fin[0], bf16) for fin, (*_, direct) in zip(fins, parts)],
            pltpu.SemaphoreType.DMA((k, team)),
            pltpu.SemaphoreType.DMA((k, team)),
            pltpu.SemaphoreType.DMA((k, n)),
            pltpu.SemaphoreType.DMA((k, n)),
            pltpu.SemaphoreType.DMA((k, n_rj)),
            pltpu.SemaphoreType.DMA((k, n_rj)),
        ],
        compiler_params=pltpu.CompilerParams(
            collective_id=0, has_side_effects=True, vmem_limit_bytes=40 << 20
        ),
    )(
        *[pltpu.with_memory_space_constraint(x, pltpu.HBM) for x in (*pre, *post)]
    )
    update = pl.pallas_call(
        finish,
        out_shape=jax.ShapeDtypeStruct((spots, w_out.shape[1]), bf16),
        in_specs=[vmem] * (4 + k),
        out_specs=pl.BlockSpec(memory_space=pl.ANY),
        scratch_shapes=[
            pltpu.VMEM((END_STEPS, spots // END_STEPS, w_out.shape[1]), bf16),
            pltpu.SemaphoreType.DMA((END_STEPS,)),
        ],
        compiler_params=pltpu.CompilerParams(vmem_limit_bytes=12 << 20),
    )(*[pltpu.with_memory_space_constraint(x, pltpu.VMEM) for x in handed])
    return update.reshape(rows, cols, w_out.shape[1])


def solution(mesh):
    n_ri, n_rj = mesh.shape["ri"], mesh.shape["rj"]
    return jax.shard_map(
        lambda *args: local(n_ri, n_rj, *args),
        mesh=mesh,
        in_specs=(P("ri", "rj", None), P(), P(), P(), P(), P(), P(), P()),
        out_specs=P("ri", "rj", None),
        check_vma=False,
    )
```

```python
import functools

import jax
import jax.numpy as jnp
from jax import lax
from jax.experimental import pallas as pl
from jax.experimental.pallas import tpu as pltpu
from jax.sharding import PartitionSpec as P

MESH = pl.DeviceIdType.MESH
LANES = 128
STEPS = 5
NORM_STEPS = 5
END_STEPS = 5
LAG = 2
AHEAD = 8


def plan(n_ri, n_rj, hidden):
    side = n_ri // 2
    per = hidden // (side * n_rj)
    if per == 8 and n_ri % 4 == 0:
        sizes = [(2, False, False), (2, False, True), (4, False, True)]
    elif per > 1:
        sizes = [(per // 2, False, True)] * 2
    else:
        sizes = [(per, False, True)]
    parts, first = [], 0
    for own, inner, direct in sizes:
        oc = side // 2 if inner else side
        parts.append((own, first, oc, inner, direct))
        first += own * oc * n_rj
    return parts


def shifted(vregs, start):
    at, by = divmod(start, LANES)
    if by == 0:
        return vregs[at]
    return pltpu.roll(vregs[at], LANES - by, 1)


def body(n_ri, n_rj, rows, cols, parts, *refs):
    np_ = len(parts)
    fetched, kept = refs[:5], refs[5:8]
    gate_s, *held = refs[8:12]
    fin_s = refs[12 : 12 + np_]
    pair, gain, bias, w_in, w_gate, flat_s, ab_s, sum_s, g_s, b_s, o_s, in_sem = refs[
        12 + np_ : 24 + np_
    ]
    x_s, recv_s, t_s, got_s, fwd_s = (
        refs[24 + (i + 1) * np_ : 24 + (i + 2) * np_] for i in range(5)
    )
    send1, recv1, send2, recv2, send3, recv3 = refs[24 + 6 * np_ :]

    spots = rows * cols
    side = n_ri // 2
    team = side * n_rj
    depth = side * rows
    hidden = w_in.shape[1] // 4
    halves = cols // rows
    ri, rj = lax.axis_index("ri"), lax.axis_index("rj")
    half = ri // side
    base = half * side
    seat = (ri - base) * n_rj + rj
    me = ri * n_rj + rj
    n = n_ri * n_rj
    low = jnp.where(half == 0, side // 2, 0)
    is_inner = jnp.logical_and(ri - base >= low, ri - base < low + side // 2)
    vregs_n = spots // LANES

    fetches = [
        pltpu.make_async_copy(src, dst, in_sem.at[i])
        for i, (src, dst) in enumerate(
            zip((*fetched, *kept), (pair, gain, bias, w_in, w_gate, *held))
        )
    ]
    for fetch in fetches:
        fetch.start()

    barrier = pltpu.get_barrier_semaphore()
    pl.semaphore_signal(
        barrier, inc=1, device_id=(lax.rem(ri + side, n_ri), rj), device_id_type=MESH
    )

    def greet(d, _):
        to = lax.rem(seat + team - d, team)
        pl.semaphore_signal(
            barrier, inc=1, device_id=(base + to // n_rj, lax.rem(to, n_rj)), device_id_type=MESH
        )
        return _

    lax.fori_loop(1, team, greet, 0)

    for fetch in fetches:
        fetch.wait()
    wt = w_in[...].T
    step = spots // STEPS

    fine = spots // NORM_STEPS

    def norm_in(i, _):
        at = pl.multiple_of(i * fine, LANES)
        x = pair[pl.ds(at, fine), :].astype(jnp.float32)
        mean = jnp.mean(x, axis=-1, keepdims=True)
        centered = x - mean
        var = jnp.mean(centered * centered, axis=-1, keepdims=True)
        flat = (centered * lax.rsqrt(var + 1e-05) * gain[...] + bias[...]).astype(jnp.bfloat16)
        flat_s[pl.ds(at, fine), :] = flat
        return _

    lax.fori_loop(0, NORM_STEPS, norm_in, 0, unroll=5)

    def plane(t):
        return base + low if parts[t][3] else base

    def owner_seat(t):
        return (ri - plane(t)) * n_rj + rj

    def owns(t, f):
        if parts[t][3]:
            pl.when(is_inner)(f)
        else:
            f()

    def copy_in(t, e, src):
        return pltpu.make_async_remote_copy(
            src_ref=x_s[t].at[e], dst_ref=recv_s[t].at[src], send_sem=send1.at[t, e],
            recv_sem=recv1.at[t, src], device_id=(plane(t) + e // n_rj, lax.rem(e, n_rj)),
            device_id_type=MESH,
        )

    def keep_in(t):
        return pltpu.make_async_copy(
            x_s[t].at[owner_seat(t)], recv_s[t].at[seat], send1.at[t, owner_seat(t)]
        )

    def my_slot(t):
        return half * parts[t][2] + ri - plane(t)

    def copy_z(t, d, slot):
        return pltpu.make_async_remote_copy(
            src_ref=t_s[t].at[d], dst_ref=got_s[t].at[slot], send_sem=send2.at[t, d],
            recv_sem=recv2.at[t, slot], device_id=(d, rj), device_id_type=MESH,
        )

    def keep_z(t):
        return pltpu.make_async_copy(t_s[t].at[ri], got_s[t].at[my_slot(t)], send2.at[t, ri])

    def copy_all(t, d, slot):
        return pltpu.make_async_remote_copy(
            src_ref=t_s[t].at[d], dst_ref=got_s[t].at[slot], send_sem=send2.at[t, d],
            recv_sem=recv2.at[t, slot], device_id=(d // n_rj, lax.rem(d, n_rj)),
            device_id_type=MESH,
        )

    def all_slot(t):
        return half * parts[t][2] * n_rj + owner_seat(t)

    def keep_all(t):
        return pltpu.make_async_copy(t_s[t].at[me], got_s[t].at[all_slot(t)], send2.at[t, me])

    def copy_xy(t, q, src):
        return pltpu.make_async_remote_copy(
            src_ref=fwd_s[t].at[q], dst_ref=fin_s[t].at[src], send_sem=send3.at[t, q],
            recv_sem=recv3.at[t, src], device_id=(ri, q), device_id_type=MESH,
        )

    def keep_xy(t):
        return pltpu.make_async_copy(fwd_s[t].at[rj], fin_s[t].at[rj], send3.at[t, rj])

    def project(t):
        own, first, oc, *_ = parts[t]
        wide = own * oc * n_rj
        each = 8 // own
        w = jnp.concatenate(
            [wt[g * hidden + first : g * hidden + first + wide] for g in range(4)], axis=0
        )

        def one(i, _):
            at = pl.multiple_of(i * step, LANES)
            proj = lax.dot_general(
                w, flat_s[pl.ds(at, step), :], (((1,), (1,)), ((), ())),
                preferred_element_type=jnp.float32,
            )
            ab_s[0, :wide, pl.ds(at, step)] = jax.nn.sigmoid(proj[wide : 2 * wide]) * proj[:wide]
            ab_s[1, :wide, pl.ds(at, step)] = (
                jax.nn.sigmoid(proj[3 * wide :]) * proj[2 * wide : 3 * wide]
            )
            return _

        lax.fori_loop(0, STEPS, one, 0, unroll=5)

        def split(p, _):
            at = pl.multiple_of(p * 8, 8)
            a8, b8 = ab_s[0, pl.ds(at, 8), :], ab_s[1, pl.ds(at, 8), :]
            for k in range(each):
                pick = slice(k * own, (k + 1) * own)
                turn = p * each + k
                x_s[t][lax.rem(turn, oc) * n_rj + turn // oc] = jnp.concatenate(
                    [a8[pick], b8[pick]], axis=0
                ).astype(jnp.bfloat16)
            return _

        lax.fori_loop(0, wide // 8, split, 0)

    def others(t, f):
        owners, mine = parts[t][2] * n_rj, owner_seat(t)

        def one(d, _):
            e = lax.rem((seat // (owners // 2) + 1 + d // (owners // 2)) * (owners // 2) + lax.rem(seat + d, owners // 2), owners)

            @pl.when(e != mine)
            def go():
                f(e)

            return _

        lax.fori_loop(0, owners, one, 0)

    def publish(t):
        project(t)
        if t == 0:
            pl.semaphore_wait(barrier, team)
        others(t, lambda e: copy_in(t, e, seat).start())
        owns(t, lambda: keep_in(t).start())

    for t in range(min(AHEAD, np_)):
        publish(t)

    def gates(i, _):
        at = pl.multiple_of(i * step, LANES)
        gate_s[pl.ds(at, step), :] = jax.nn.sigmoid(
            jnp.dot(flat_s[pl.ds(at, step), :], w_gate[...], preferred_element_type=jnp.float32)
        ).astype(jnp.bfloat16)
        return _


    lane8 = lax.broadcasted_iota(jnp.int32, (8, LANES), 1)

    def work(t):
        own, direct = parts[t][0], parts[t][4]
        merge = 4 // own
        deep = depth // merge
        ranks = side // merge

        def take(turn, _):
            lot = ranks * n_rj
            side_lot = team // 2
            if lot == team:
                at = lax.rem((seat // side_lot + 1 + turn // side_lot) * side_lot + lax.rem(seat + team - turn, side_lot), team)
            else:
                at = lax.rem(seat + team - turn, lot)
            r, j = at // n_rj, lax.rem(at, n_rj)
            for b in range(merge):
                src = (r + b * ranks) * n_rj + j

                @pl.when(src == seat)
                def kept():
                    keep_in(t).wait()

                @pl.when(src != seat)
                def came():
                    copy_in(t, 0, src).wait_recv()

            blocks = [
                recv_s[t][(r + b * ranks) * n_rj + j].astype(jnp.float32) for b in range(merge)
            ]
            wide = jnp.concatenate(blocks, axis=0) if merge > 1 else blocks[0]
            vregs = [wide[:, v * LANES : (v + 1) * LANES] for v in range(vregs_n)]
            for k in range(rows):
                start = k * cols
                val = shifted(vregs, start)
                have = LANES - start % LANES
                if have < cols:
                    val = jnp.where(
                        lane8 < have, val, pltpu.roll(vregs[start // LANES + 1], have, 1)
                    )
                g_s[j, pl.ds(r * rows + k, 8, stride=deep), :] = val
            return _

        lax.fori_loop(0, ranks * n_rj, take, 0)

        def operand(j, s):
            return [
                g_s[j, (b * 2 * own + s) * deep : (b * 2 * own + s + 1) * deep, :].astype(
                    jnp.bfloat16
                )
                for b in range(merge)
            ]

        for c in range(own):
            for q in range(n_rj):
                b_s[c, :, q * LANES : (q + 1) * LANES] = jnp.concatenate(
                    operand(q, own + c), axis=0
                )

        def emit(pp, _):
            p = lax.rem(pp + (1 - half) * (n_rj // 2), n_rj)
            for c in range(own):
                product = lax.dot_general(
                    jnp.concatenate(operand(p, c), axis=0), b_s[c], (((0,), (0,)), ((), ())),
                    preferred_element_type=jnp.float32,
                )
                for q in range(n_rj):
                    if direct:
                        at = lax.rem(q + n_rj - rj, n_rj) * own + c
                    else:
                        at = c * n_rj + q
                    o_s[pl.ds(pl.multiple_of(at * LANES, LANES), LANES), :] = product[
                        :, q * LANES : (q + 1) * LANES
                    ]

            def deliver(h, _):
                d = p * halves + h
                slabs = []
                for g in range(own * n_rj // 8):
                    got = [
                        o_s[pl.ds(g * 8 * LANES + h * rows + r, 8, stride=LANES), :]
                        for r in range(rows)
                    ]
                    pieces = []
                    for v in range(vregs_n):
                        piece = None
                        for r in range(
                            (v * LANES) // cols, min(rows, ((v + 1) * LANES - 1) // cols + 1)
                        ):
                            at = r * cols - v * LANES
                            val = pltpu.roll(got[r], at % LANES, 1) if at % LANES else got[r]
                            piece = val if piece is None else jnp.where(lane8 >= at, val, piece)
                        pieces.append(piece)
                    slabs.append(jnp.concatenate(pieces, axis=1))
                if direct:
                    for turn in range(n_rj):
                        to = d * n_rj + lax.rem(turn + rj, n_rj)
                        at = turn * own
                        t_s[t][to] = slabs[at // 8][at % 8 : at % 8 + own].astype(jnp.bfloat16)

                        @pl.when(to != me)
                        def go(to=to):
                            copy_all(t, to, all_slot(t)).start()

                    return _

                slab = jnp.concatenate(slabs, axis=0) if len(slabs) > 1 else slabs[0]
                t_s[t][d] = slab.astype(jnp.bfloat16)

                @pl.when(d != ri)
                def start():
                    copy_z(t, d, my_slot(t)).start()

                return _

            lax.fori_loop(0, halves, deliver, 0)
            return _

        lax.fori_loop(0, n_rj, emit, 0)
        (keep_all if direct else keep_z)(t).start()

    def total(t):
        own, first, oc, inner, _ = parts[t]
        mine = my_slot(t)

        def arrive(s, _):
            go = s != mine
            if inner:
                go = jnp.logical_or(go, jnp.logical_not(is_inner))

            @pl.when(go)
            def wait():
                copy_z(t, 0, s).wait_recv()

            return _

        lax.fori_loop(0, 2 * oc, arrive, 0)
        owns(t, lambda: keep_z(t).wait())
        tall = own * n_rj

        def add(o, _):
            both = got_s[t][o].astype(jnp.float32) + got_s[t][oc + o].astype(jnp.float32)
            at = pl.multiple_of(o * tall, 8)
            for v in range(vregs_n):
                sum_s[v, pl.ds(at, tall), :] = both[:, v * LANES : (v + 1) * LANES]
            return _

        lax.fori_loop(0, oc, add, 0)

        def forward(d, _):
            q = lax.rem(rj + 1 + d, n_rj)
            fwd_s[t][q] = jnp.concatenate(
                [sum_s[v, pl.ds(q, oc * own, stride=n_rj), :] for v in range(vregs_n)], axis=1
            ).astype(jnp.bfloat16)

            @pl.when(q != rj)
            def start():
                copy_xy(t, q, rj).start()

            return _

        lax.fori_loop(0, n_rj, forward, 0)
        keep_xy(t).start()

    for t in range(np_):
        owns(t, lambda t=t: work(t))
        if t + AHEAD < np_:
            publish(t + AHEAD)
        if t >= LAG and not parts[t - LAG][4]:
            total(t - LAG)
    lax.fori_loop(0, STEPS, gates, 0)

    for t in range(max(np_ - LAG, 0), np_):
        if not parts[t][4]:
            total(t)

    def settle(t):
        def drain():
            def sent(d, _):
                @pl.when(d != ri)
                def wait():
                    copy_z(t, d, my_slot(t)).wait_send()

                return _

            lax.fori_loop(0, n_ri, sent, 0)

        owns(t, drain)

        def last(d, _):
            q = lax.rem(rj + d, n_rj)
            copy_xy(t, q, rj).wait_send()
            copy_xy(t, 0, q).wait_recv()
            return _

        lax.fori_loop(1, n_rj, last, 0)
        keep_xy(t).wait()

    def gather(t):
        own, first, oc, inner, _ = parts[t]
        owners, mine, each = oc * n_rj, all_slot(t), 8 // own

        def drain():
            def sent(d, _):
                copy_all(t, lax.rem(me + d, n), mine).wait_send()
                return _

            lax.fori_loop(1, n, sent, 0)
            keep_all(t).wait()

        owns(t, drain)

        def arrive(s):
            go = s != mine
            if inner:
                go = jnp.logical_or(go, jnp.logical_not(is_inner))

            @pl.when(go)
            def wait():
                copy_all(t, 0, s).wait_recv()

        def merge(p, _):
            sums = []
            for k in range(each):
                turn = p * each + k
                e = lax.rem(turn, oc) * n_rj + turn // oc
                arrive(e)
                arrive(owners + e)
                sums.append(
                    got_s[t][e].astype(jnp.float32) + got_s[t][owners + e].astype(jnp.float32)
                )
            fin_s[t][0, pl.ds(pl.multiple_of(p * 8, 8), 8), :] = jnp.concatenate(sums, axis=0)
            return _

        lax.fori_loop(0, own * owners // 8, merge, 0)

    for t in range(np_):
        others(t, lambda e, t=t: copy_in(t, e, seat).wait_send())

        if parts[t][4]:
            gather(t)
        else:
            settle(t)


def finish(gate, out_gain, out_bias, w_out, *refs):
    *parts, upd, chunk_s, sem = refs
    hidden = w_out.shape[0]
    spots = gate.shape[0]
    step = spots // END_STEPS

    def column(row):
        tall = jnp.broadcast_to(row[...], (LANES, hidden)).T
        return jnp.concatenate([tall] * (step // LANES), axis=1)

    post_gain, post_bias = column(out_gain), column(out_bias)

    def put(i):
        return pltpu.make_async_copy(
            chunk_s.at[i], upd.at[pl.ds(pl.multiple_of(i * step, LANES), step), :], sem.at[i]
        )

    def one(i, _):
        at = pl.multiple_of(i * step, LANES)
        x = jnp.concatenate(
            [
                part[q, :, pl.ds(at, step)].astype(jnp.float32)
                for part in parts
                for q in range(part.shape[0])
            ],
            axis=0,
        )
        mean = jnp.mean(x, axis=0, keepdims=True)
        centered = x - mean
        var = jnp.mean(centered * centered, axis=0, keepdims=True)
        normed = (centered * lax.rsqrt(var + 1e-05) * post_gain + post_bias).astype(jnp.bfloat16)
        mixed = lax.dot_general(
            normed, w_out[...], (((0,), (0,)), ((), ())), preferred_element_type=jnp.float32
        )
        chunk_s[i] = (gate[pl.ds(at, step), :].astype(jnp.float32) * mixed).astype(jnp.bfloat16)
        put(i).start()
        return _

    lax.fori_loop(0, END_STEPS, one, 0, unroll=5)

    def done(i, _):
        put(i).wait()
        return _

    lax.fori_loop(0, END_STEPS, done, 0)


def local(n_ri, n_rj, pair, in_gain, in_bias, w_in, w_gate, out_gain, out_bias, w_out):
    rows, cols, chans = pair.shape
    hidden = w_out.shape[0]
    team = n_ri // 2 * n_rj
    spots = rows * cols
    depth = (n_ri // 2) * rows
    parts = plan(n_ri, n_rj, hidden)
    most = max(own for own, *_ in parts)
    col = max(own * oc for own, _, oc, *_ in parts)
    vmem = pl.BlockSpec(memory_space=pltpu.VMEM)
    bf16, f32 = jnp.bfloat16, jnp.float32
    k = len(parts)
    pre = (pair.reshape(spots, chans), in_gain[None], in_bias[None], w_in, w_gate)
    post = (out_gain[None], out_bias[None], w_out)
    fins = [
        ((1, n_rj * own * oc, spots), f32) if direct else ((n_rj, own * oc, spots), bf16)
        for own, _, oc, _, direct in parts
    ]
    n = n_ri * n_rj
    tiny = (1, 8, LANES)
    handed = pl.pallas_call(
        functools.partial(body, n_ri, n_rj, rows, cols, parts),
        out_shape=(
            pltpu.VMEM((spots, chans), bf16),
            *[pltpu.VMEM(x.shape, x.dtype) for x in post],
            *[pltpu.VMEM(*fin) for fin in fins],
        ),
        in_specs=[pl.BlockSpec(memory_space=pl.ANY)] * 8,
        out_specs=[vmem] * (4 + k),
        scratch_shapes=[
            *[pltpu.VMEM(x.shape, x.dtype) for x in pre],
            pltpu.VMEM((spots, chans), bf16),
            pltpu.VMEM((2, col * n_rj, spots), f32),
            pltpu.VMEM((spots // LANES, col * n_rj, LANES), f32),
            pltpu.VMEM((n_rj, 2 * most * depth, LANES), f32),
            pltpu.VMEM((most, depth, n_rj * LANES), bf16),
            pltpu.VMEM((most * n_rj * LANES, LANES), f32),
            pltpu.SemaphoreType.DMA((8,)),
            *[pltpu.VMEM((oc * n_rj, 2 * own, spots), bf16) for own, _, oc, *_ in parts],
            *[pltpu.VMEM((team, 2 * own, spots), bf16) for own, _, oc, *_ in parts],
            *[
                pltpu.VMEM((n, own, spots) if direct else (n_ri, own * n_rj, spots), bf16)
                for own, _, oc, _, direct in parts
            ],
            *[
                pltpu.VMEM(
                    (2 * oc * n_rj, own, spots) if direct else (2 * oc, own * n_rj, spots), bf16
                )
                for own, _, oc, _, direct in parts
            ],
            *[pltpu.VMEM(tiny if direct else fin[0], bf16) for fin, (*_, direct) in zip(fins, parts)],
            pltpu.SemaphoreType.DMA((k, team)),
            pltpu.SemaphoreType.DMA((k, team)),
            pltpu.SemaphoreType.DMA((k, n)),
            pltpu.SemaphoreType.DMA((k, n)),
            pltpu.SemaphoreType.DMA((k, n_rj)),
            pltpu.SemaphoreType.DMA((k, n_rj)),
        ],
        compiler_params=pltpu.CompilerParams(
            collective_id=0, has_side_effects=True, vmem_limit_bytes=40 << 20
        ),
    )(
        *[pltpu.with_memory_space_constraint(x, pltpu.HBM) for x in (*pre, *post)]
    )
    update = pl.pallas_call(
        finish,
        out_shape=jax.ShapeDtypeStruct((spots, w_out.shape[1]), bf16),
        in_specs=[vmem] * (4 + k),
        out_specs=pl.BlockSpec(memory_space=pl.ANY),
        scratch_shapes=[
            pltpu.VMEM((END_STEPS, spots // END_STEPS, w_out.shape[1]), bf16),
            pltpu.SemaphoreType.DMA((END_STEPS,)),
        ],
        compiler_params=pltpu.CompilerParams(vmem_limit_bytes=12 << 20),
    )(*[pltpu.with_memory_space_constraint(x, pltpu.VMEM) for x in handed])
    return update.reshape(rows, cols, w_out.shape[1])


def solution(mesh):
    n_ri, n_rj = mesh.shape["ri"], mesh.shape["rj"]
    return jax.shard_map(
        lambda *args: local(n_ri, n_rj, *args),
        mesh=mesh,
        in_specs=(P("ri", "rj", None), P(), P(), P(), P(), P(), P(), P()),
        out_specs=P("ri", "rj", None),
        check_vma=False,
    )
```

```python
import functools

import jax
import jax.numpy as jnp
from jax import lax
from jax.experimental import pallas as pl
from jax.experimental.pallas import tpu as pltpu
from jax.sharding import PartitionSpec as P

MESH = pl.DeviceIdType.MESH
LANES = 128
STEPS = 5
NORM_STEPS = 5
END_STEPS = 5
LAG = 2
AHEAD = 8


def plan(n_ri, n_rj, hidden):
    side = n_ri // 2
    per = hidden // (side * n_rj)
    if per == 8 and n_ri % 4 == 0:
        sizes = [(2, False, False), (2, False, True), (4, False, True)]
    elif per > 1:
        sizes = [(per // 2, False, True)] * 2
    else:
        sizes = [(per, False, True)]
    parts, first = [], 0
    for own, inner, direct in sizes:
        oc = side // 2 if inner else side
        parts.append((own, first, oc, inner, direct))
        first += own * oc * n_rj
    return parts


def shifted(vregs, start):
    at, by = divmod(start, LANES)
    if by == 0:
        return vregs[at]
    return pltpu.roll(vregs[at], LANES - by, 1)


def body(n_ri, n_rj, rows, cols, parts, *refs):
    np_ = len(parts)
    fetched, kept = refs[:5], refs[5:8]
    gate_s, *held = refs[8:12]
    fin_s = refs[12 : 12 + np_]
    pair, gain, bias, w_in, w_gate, flat_s, ab_s, sum_s, g_s, b_s, o_s, in_sem = refs[
        12 + np_ : 24 + np_
    ]
    x_s, recv_s, t_s, got_s, fwd_s = (
        refs[24 + (i + 1) * np_ : 24 + (i + 2) * np_] for i in range(5)
    )
    send1, recv1, send2, recv2, send3, recv3 = refs[24 + 6 * np_ :]

    spots = rows * cols
    side = n_ri // 2
    team = side * n_rj
    depth = side * rows
    hidden = w_in.shape[1] // 4
    halves = cols // rows
    ri, rj = lax.axis_index("ri"), lax.axis_index("rj")
    half = ri // side
    base = half * side
    seat = (ri - base) * n_rj + rj
    me = ri * n_rj + rj
    n = n_ri * n_rj
    low = jnp.where(half == 0, side // 2, 0)
    is_inner = jnp.logical_and(ri - base >= low, ri - base < low + side // 2)
    vregs_n = spots // LANES

    fetches = [
        pltpu.make_async_copy(src, dst, in_sem.at[i])
        for i, (src, dst) in enumerate(
            zip((*fetched, *kept), (pair, gain, bias, w_in, w_gate, *held))
        )
    ]
    for fetch in fetches:
        fetch.start()

    barrier = pltpu.get_barrier_semaphore()
    pl.semaphore_signal(
        barrier, inc=1, device_id=(lax.rem(ri + side, n_ri), rj), device_id_type=MESH
    )

    def greet(d, _):
        to = lax.rem(seat + team - d, team)
        pl.semaphore_signal(
            barrier, inc=1, device_id=(base + to // n_rj, lax.rem(to, n_rj)), device_id_type=MESH
        )
        return _

    lax.fori_loop(1, team, greet, 0)

    for fetch in fetches:
        fetch.wait()
    wt = w_in[...].T
    step = spots // STEPS

    fine = spots // NORM_STEPS

    def norm_in(i, _):
        at = pl.multiple_of(i * fine, LANES)
        x = pair[pl.ds(at, fine), :].astype(jnp.float32)
        mean = jnp.mean(x, axis=-1, keepdims=True)
        centered = x - mean
        var = jnp.mean(centered * centered, axis=-1, keepdims=True)
        flat = (centered * lax.rsqrt(var + 1e-05) * gain[...] + bias[...]).astype(jnp.bfloat16)
        flat_s[pl.ds(at, fine), :] = flat
        return _

    lax.fori_loop(0, NORM_STEPS, norm_in, 0, unroll=5)

    def plane(t):
        return base + low if parts[t][3] else base

    def owner_seat(t):
        return (ri - plane(t)) * n_rj + rj

    def owns(t, f):
        if parts[t][3]:
            pl.when(is_inner)(f)
        else:
            f()

    def copy_in(t, e, src):
        return pltpu.make_async_remote_copy(
            src_ref=x_s[t].at[e], dst_ref=recv_s[t].at[src], send_sem=send1.at[t, e],
            recv_sem=recv1.at[t, src], device_id=(plane(t) + e // n_rj, lax.rem(e, n_rj)),
            device_id_type=MESH,
        )

    def keep_in(t):
        return pltpu.make_async_copy(
            x_s[t].at[owner_seat(t)], recv_s[t].at[seat], send1.at[t, owner_seat(t)]
        )

    def my_slot(t):
        return half * parts[t][2] + ri - plane(t)

    def copy_z(t, d, slot):
        return pltpu.make_async_remote_copy(
            src_ref=t_s[t].at[d], dst_ref=got_s[t].at[slot], send_sem=send2.at[t, d],
            recv_sem=recv2.at[t, slot], device_id=(d, rj), device_id_type=MESH,
        )

    def keep_z(t):
        return pltpu.make_async_copy(t_s[t].at[ri], got_s[t].at[my_slot(t)], send2.at[t, ri])

    def copy_all(t, d, slot):
        return pltpu.make_async_remote_copy(
            src_ref=t_s[t].at[d], dst_ref=got_s[t].at[slot], send_sem=send2.at[t, d],
            recv_sem=recv2.at[t, slot], device_id=(d // n_rj, lax.rem(d, n_rj)),
            device_id_type=MESH,
        )

    def all_slot(t):
        return half * parts[t][2] * n_rj + owner_seat(t)

    def keep_all(t):
        return pltpu.make_async_copy(t_s[t].at[me], got_s[t].at[all_slot(t)], send2.at[t, me])

    def copy_xy(t, q, src):
        return pltpu.make_async_remote_copy(
            src_ref=fwd_s[t].at[q], dst_ref=fin_s[t].at[src], send_sem=send3.at[t, q],
            recv_sem=recv3.at[t, src], device_id=(ri, q), device_id_type=MESH,
        )

    def keep_xy(t):
        return pltpu.make_async_copy(fwd_s[t].at[rj], fin_s[t].at[rj], send3.at[t, rj])

    def project(t):
        own, first, oc, *_ = parts[t]
        wide = own * oc * n_rj
        each = 8 // own
        w = jnp.concatenate(
            [wt[g * hidden + first : g * hidden + first + wide] for g in range(4)], axis=0
        )

        def one(i, _):
            at = pl.multiple_of(i * step, LANES)
            proj = lax.dot_general(
                w, flat_s[pl.ds(at, step), :], (((1,), (1,)), ((), ())),
                preferred_element_type=jnp.float32,
            )
            ab_s[0, :wide, pl.ds(at, step)] = jax.nn.sigmoid(proj[wide : 2 * wide]) * proj[:wide]
            ab_s[1, :wide, pl.ds(at, step)] = (
                jax.nn.sigmoid(proj[3 * wide :]) * proj[2 * wide : 3 * wide]
            )
            return _

        lax.fori_loop(0, STEPS, one, 0, unroll=5)

        def split(p, _):
            at = pl.multiple_of(p * 8, 8)
            a8, b8 = ab_s[0, pl.ds(at, 8), :], ab_s[1, pl.ds(at, 8), :]
            for k in range(each):
                pick = slice(k * own, (k + 1) * own)
                turn = p * each + k
                x_s[t][lax.rem(turn, oc) * n_rj + turn // oc] = jnp.concatenate(
                    [a8[pick], b8[pick]], axis=0
                ).astype(jnp.bfloat16)
            return _

        lax.fori_loop(0, wide // 8, split, 0)

    def others(t, f):
        owners, mine = parts[t][2] * n_rj, owner_seat(t)

        def one(d, _):
            e = lax.rem((seat // (owners // 2) + 1 + d // (owners // 2)) * (owners // 2) + lax.rem(seat + d, owners // 2), owners)

            @pl.when(e != mine)
            def go():
                f(e)

            return _

        lax.fori_loop(0, owners, one, 0)

    def publish(t):
        project(t)
        if t == 0:
            pl.semaphore_wait(barrier, team)
        others(t, lambda e: copy_in(t, e, seat).start())
        owns(t, lambda: keep_in(t).start())

    for t in range(min(AHEAD, np_)):
        publish(t)

    def gates(i, _):
        at = pl.multiple_of(i * step, LANES)
        gate_s[pl.ds(at, step), :] = jax.nn.sigmoid(
            jnp.dot(flat_s[pl.ds(at, step), :], w_gate[...], preferred_element_type=jnp.float32)
        ).astype(jnp.bfloat16)
        return _


    lane8 = lax.broadcasted_iota(jnp.int32, (8, LANES), 1)

    def work(t):
        own, direct = parts[t][0], parts[t][4]
        merge = 4 // own
        deep = depth // merge
        ranks = side // merge

        def take(turn, _):
            lot = ranks * n_rj
            side_lot = team // 2
            if lot == team:
                at = lax.rem((seat // side_lot + 1 + turn // side_lot) * side_lot + lax.rem(seat + team - turn, side_lot), team)
            else:
                at = lax.rem(seat + team - turn, lot)
            r, j = at // n_rj, lax.rem(at, n_rj)
            for b in range(merge):
                src = (r + b * ranks) * n_rj + j

                @pl.when(src == seat)
                def kept():
                    keep_in(t).wait()

                @pl.when(src != seat)
                def came():
                    copy_in(t, 0, src).wait_recv()

            blocks = [
                recv_s[t][(r + b * ranks) * n_rj + j].astype(jnp.float32) for b in range(merge)
            ]
            wide = jnp.concatenate(blocks, axis=0) if merge > 1 else blocks[0]
            vregs = [wide[:, v * LANES : (v + 1) * LANES] for v in range(vregs_n)]
            for k in range(rows):
                start = k * cols
                val = shifted(vregs, start)
                have = LANES - start % LANES
                if have < cols:
                    val = jnp.where(
                        lane8 < have, val, pltpu.roll(vregs[start // LANES + 1], have, 1)
                    )
                g_s[j, pl.ds(r * rows + k, 8, stride=deep), :] = val
            return _

        lax.fori_loop(0, ranks * n_rj, take, 0)

        def operand(j, s):
            return [
                g_s[j, (b * 2 * own + s) * deep : (b * 2 * own + s + 1) * deep, :].astype(
                    jnp.bfloat16
                )
                for b in range(merge)
            ]

        for c in range(own):
            for q in range(n_rj):
                b_s[c, :, q * LANES : (q + 1) * LANES] = jnp.concatenate(
                    operand(q, own + c), axis=0
                )

        def emit(pp, _):
            p = lax.rem(pp + (1 - half) * (n_rj // 2), n_rj)
            for c in range(own):
                product = lax.dot_general(
                    jnp.concatenate(operand(p, c), axis=0), b_s[c], (((0,), (0,)), ((), ())),
                    preferred_element_type=jnp.float32,
                )
                for q in range(n_rj):
                    if direct:
                        at = lax.rem(q + n_rj - rj, n_rj) * own + c
                    else:
                        at = c * n_rj + q
                    o_s[pl.ds(pl.multiple_of(at * LANES, LANES), LANES), :] = product[
                        :, q * LANES : (q + 1) * LANES
                    ]

            def deliver(h, _):
                d = p * halves + h
                slabs = []
                for g in range(own * n_rj // 8):
                    got = [
                        o_s[pl.ds(g * 8 * LANES + h * rows + r, 8, stride=LANES), :]
                        for r in range(rows)
                    ]
                    pieces = []
                    for v in range(vregs_n):
                        piece = None
                        for r in range(
                            (v * LANES) // cols, min(rows, ((v + 1) * LANES - 1) // cols + 1)
                        ):
                            at = r * cols - v * LANES
                            val = pltpu.roll(got[r], at % LANES, 1) if at % LANES else got[r]
                            piece = val if piece is None else jnp.where(lane8 >= at, val, piece)
                        pieces.append(piece)
                    slabs.append(jnp.concatenate(pieces, axis=1))
                if direct:
                    for turn in range(n_rj):
                        to = d * n_rj + lax.rem(turn + rj, n_rj)
                        at = turn * own
                        t_s[t][to] = slabs[at // 8][at % 8 : at % 8 + own].astype(jnp.bfloat16)

                        @pl.when(to != me)
                        def go(to=to):
                            copy_all(t, to, all_slot(t)).start()

                    return _

                slab = jnp.concatenate(slabs, axis=0) if len(slabs) > 1 else slabs[0]
                t_s[t][d] = slab.astype(jnp.bfloat16)

                @pl.when(d != ri)
                def start():
                    copy_z(t, d, my_slot(t)).start()

                return _

            lax.fori_loop(0, halves, deliver, 0)
            return _

        lax.fori_loop(0, n_rj, emit, 0)
        (keep_all if direct else keep_z)(t).start()

    def total(t):
        own, first, oc, inner, _ = parts[t]
        mine = my_slot(t)

        def arrive(s, _):
            go = s != mine
            if inner:
                go = jnp.logical_or(go, jnp.logical_not(is_inner))

            @pl.when(go)
            def wait():
                copy_z(t, 0, s).wait_recv()

            return _

        lax.fori_loop(0, 2 * oc, arrive, 0)
        owns(t, lambda: keep_z(t).wait())
        tall = own * n_rj

        def add(o, _):
            both = got_s[t][o].astype(jnp.float32) + got_s[t][oc + o].astype(jnp.float32)
            at = pl.multiple_of(o * tall, 8)
            for v in range(vregs_n):
                sum_s[v, pl.ds(at, tall), :] = both[:, v * LANES : (v + 1) * LANES]
            return _

        lax.fori_loop(0, oc, add, 0)

        def forward(d, _):
            q = lax.rem(rj + 1 + d, n_rj)
            fwd_s[t][q] = jnp.concatenate(
                [sum_s[v, pl.ds(q, oc * own, stride=n_rj), :] for v in range(vregs_n)], axis=1
            ).astype(jnp.bfloat16)

            @pl.when(q != rj)
            def start():
                copy_xy(t, q, rj).start()

            return _

        lax.fori_loop(0, n_rj, forward, 0, unroll=2)
        keep_xy(t).start()

    for t in range(np_):
        owns(t, lambda t=t: work(t))
        if t + AHEAD < np_:
            publish(t + AHEAD)
        if t >= LAG and not parts[t - LAG][4]:
            total(t - LAG)
    lax.fori_loop(0, STEPS, gates, 0)

    for t in range(max(np_ - LAG, 0), np_):
        if not parts[t][4]:
            total(t)

    def settle(t):
        def drain():
            def sent(d, _):
                @pl.when(d != ri)
                def wait():
                    copy_z(t, d, my_slot(t)).wait_send()

                return _

            lax.fori_loop(0, n_ri, sent, 0)

        owns(t, drain)

        def last(d, _):
            q = lax.rem(rj + d, n_rj)
            copy_xy(t, q, rj).wait_send()
            copy_xy(t, 0, q).wait_recv()
            return _

        lax.fori_loop(1, n_rj, last, 0)
        keep_xy(t).wait()

    def gather(t):
        own, first, oc, inner, _ = parts[t]
        owners, mine, each = oc * n_rj, all_slot(t), 8 // own

        def drain():
            def sent(d, _):
                copy_all(t, lax.rem(me + d, n), mine).wait_send()
                return _

            lax.fori_loop(1, n, sent, 0)
            keep_all(t).wait()

        owns(t, drain)

        def arrive(s):
            go = s != mine
            if inner:
                go = jnp.logical_or(go, jnp.logical_not(is_inner))

            @pl.when(go)
            def wait():
                copy_all(t, 0, s).wait_recv()

        def merge(p, _):
            sums = []
            for k in range(each):
                turn = p * each + k
                e = lax.rem(turn, oc) * n_rj + turn // oc
                arrive(e)
                arrive(owners + e)
                sums.append(
                    got_s[t][e].astype(jnp.float32) + got_s[t][owners + e].astype(jnp.float32)
                )
            fin_s[t][0, pl.ds(pl.multiple_of(p * 8, 8), 8), :] = jnp.concatenate(sums, axis=0)
            return _

        lax.fori_loop(0, own * owners // 8, merge, 0, unroll=4)

    for t in range(np_):
        others(t, lambda e, t=t: copy_in(t, e, seat).wait_send())

        if parts[t][4]:
            gather(t)
        else:
            settle(t)


def finish(gate, out_gain, out_bias, w_out, *refs):
    *parts, upd, chunk_s, sem = refs
    hidden = w_out.shape[0]
    spots = gate.shape[0]
    step = spots // END_STEPS

    def column(row):
        tall = jnp.broadcast_to(row[...], (LANES, hidden)).T
        return jnp.concatenate([tall] * (step // LANES), axis=1)

    post_gain, post_bias = column(out_gain), column(out_bias)

    def put(i):
        return pltpu.make_async_copy(
            chunk_s.at[i], upd.at[pl.ds(pl.multiple_of(i * step, LANES), step), :], sem.at[i]
        )

    def one(i, _):
        at = pl.multiple_of(i * step, LANES)
        x = jnp.concatenate(
            [
                part[q, :, pl.ds(at, step)].astype(jnp.float32)
                for part in parts
                for q in range(part.shape[0])
            ],
            axis=0,
        )
        mean = jnp.mean(x, axis=0, keepdims=True)
        centered = x - mean
        var = jnp.mean(centered * centered, axis=0, keepdims=True)
        normed = (centered * lax.rsqrt(var + 1e-05) * post_gain + post_bias).astype(jnp.bfloat16)
        mixed = lax.dot_general(
            normed, w_out[...], (((0,), (0,)), ((), ())), preferred_element_type=jnp.float32
        )
        chunk_s[i] = (gate[pl.ds(at, step), :].astype(jnp.float32) * mixed).astype(jnp.bfloat16)
        put(i).start()
        return _

    lax.fori_loop(0, END_STEPS, one, 0, unroll=5)

    def done(i, _):
        put(i).wait()
        return _

    lax.fori_loop(0, END_STEPS, done, 0)


def local(n_ri, n_rj, pair, in_gain, in_bias, w_in, w_gate, out_gain, out_bias, w_out):
    rows, cols, chans = pair.shape
    hidden = w_out.shape[0]
    team = n_ri // 2 * n_rj
    spots = rows * cols
    depth = (n_ri // 2) * rows
    parts = plan(n_ri, n_rj, hidden)
    most = max(own for own, *_ in parts)
    col = max(own * oc for own, _, oc, *_ in parts)
    vmem = pl.BlockSpec(memory_space=pltpu.VMEM)
    bf16, f32 = jnp.bfloat16, jnp.float32
    k = len(parts)
    pre = (pair.reshape(spots, chans), in_gain[None], in_bias[None], w_in, w_gate)
    post = (out_gain[None], out_bias[None], w_out)
    fins = [
        ((1, n_rj * own * oc, spots), f32) if direct else ((n_rj, own * oc, spots), bf16)
        for own, _, oc, _, direct in parts
    ]
    n = n_ri * n_rj
    tiny = (1, 8, LANES)
    handed = pl.pallas_call(
        functools.partial(body, n_ri, n_rj, rows, cols, parts),
        out_shape=(
            pltpu.VMEM((spots, chans), bf16),
            *[pltpu.VMEM(x.shape, x.dtype) for x in post],
            *[pltpu.VMEM(*fin) for fin in fins],
        ),
        in_specs=[pl.BlockSpec(memory_space=pl.ANY)] * 8,
        out_specs=[vmem] * (4 + k),
        scratch_shapes=[
            *[pltpu.VMEM(x.shape, x.dtype) for x in pre],
            pltpu.VMEM((spots, chans), bf16),
            pltpu.VMEM((2, col * n_rj, spots), f32),
            pltpu.VMEM((spots // LANES, col * n_rj, LANES), f32),
            pltpu.VMEM((n_rj, 2 * most * depth, LANES), f32),
            pltpu.VMEM((most, depth, n_rj * LANES), bf16),
            pltpu.VMEM((most * n_rj * LANES, LANES), f32),
            pltpu.SemaphoreType.DMA((8,)),
            *[pltpu.VMEM((oc * n_rj, 2 * own, spots), bf16) for own, _, oc, *_ in parts],
            *[pltpu.VMEM((team, 2 * own, spots), bf16) for own, _, oc, *_ in parts],
            *[
                pltpu.VMEM((n, own, spots) if direct else (n_ri, own * n_rj, spots), bf16)
                for own, _, oc, _, direct in parts
            ],
            *[
                pltpu.VMEM(
                    (2 * oc * n_rj, own, spots) if direct else (2 * oc, own * n_rj, spots), bf16
                )
                for own, _, oc, _, direct in parts
            ],
            *[pltpu.VMEM(tiny if direct else fin[0], bf16) for fin, (*_, direct) in zip(fins, parts)],
            pltpu.SemaphoreType.DMA((k, team)),
            pltpu.SemaphoreType.DMA((k, team)),
            pltpu.SemaphoreType.DMA((k, n)),
            pltpu.SemaphoreType.DMA((k, n)),
            pltpu.SemaphoreType.DMA((k, n_rj)),
            pltpu.SemaphoreType.DMA((k, n_rj)),
        ],
        compiler_params=pltpu.CompilerParams(
            collective_id=0, has_side_effects=True, vmem_limit_bytes=40 << 20
        ),
    )(
        *[pltpu.with_memory_space_constraint(x, pltpu.HBM) for x in (*pre, *post)]
    )
    update = pl.pallas_call(
        finish,
        out_shape=jax.ShapeDtypeStruct((spots, w_out.shape[1]), bf16),
        in_specs=[vmem] * (4 + k),
        out_specs=pl.BlockSpec(memory_space=pl.ANY),
        scratch_shapes=[
            pltpu.VMEM((END_STEPS, spots // END_STEPS, w_out.shape[1]), bf16),
            pltpu.SemaphoreType.DMA((END_STEPS,)),
        ],
        compiler_params=pltpu.CompilerParams(vmem_limit_bytes=12 << 20),
    )(*[pltpu.with_memory_space_constraint(x, pltpu.VMEM) for x in handed])
    return update.reshape(rows, cols, w_out.shape[1])


def solution(mesh):
    n_ri, n_rj = mesh.shape["ri"], mesh.shape["rj"]
    return jax.shard_map(
        lambda *args: local(n_ri, n_rj, *args),
        mesh=mesh,
        in_specs=(P("ri", "rj", None), P(), P(), P(), P(), P(), P(), P()),
        out_specs=P("ri", "rj", None),
        check_vma=False,
    )
```
